256 devices in a mesh: rows: 64 (over x_lo, y, z), cols: 4 (over x_hi, core).
Axes of the slice: x: 4 (x_hi: 2, x_lo: 2; x = x_hi * 2 + x_lo), y: 4, z: 8, core: 2. Of those that a mesh axis runs over, the one named last changes fastest.
Arguments:
- l_blocks: bfloat16 [2048, 64, 1920], P(('rows', 'cols')), may hold values from -0.25 to 0.25
- s_blocks: bfloat16 [2048, 64, 1280], P('rows', None, 'cols'), may hold values from -6 to 6
- l_index: int32 [2048, 30], P(('rows', 'cols')), may hold values from 0 to 2047, as said below
- s_cols: int32 [2048, 20], replicated, may hold values from 0 to 2047, as said below
- c_index: int32 [2048, 24], P(('rows', 'cols')), may hold values from 0 to 2047, as said below
Outputs:
- product: bfloat16 [2048, 64, 1536], P(('rows', 'cols'))
The draws below stay inside these ranges and needn't reach their ends.
Inputs may be any that keep to these rules, and one draw needn't show every extreme that they name: `l_index`: the 30 entries of block-row i are distinct and lie in the window of 31 block-rows starting at max(0, min(i - 15, 2017)). `s_cols`: the entries of one block-row are distinct; those in slots p * 5 to (p + 1) * 5 - 1 are congruent to p modulo 20 // 5 and lie within 7 such columns around the block-row. `c_index`: the entries of one block-row are distinct; those in slots p * 6 to (p + 1) * 6 - 1 are congruent to p modulo 24 // 6 and lie within 16 such columns around the block-row.
All inputs are finite; a program needn't handle non-finite values.
Results may differ from the reference program's by a relative error of at most 0.001.
Values may be sent and summed in bfloat16 or wider, within the bound.
No kernel may reach another device: no remote copies, remote signals or barrier semaphores. Data moves between devices by JAX's collectives and lax.ppermute only.
A program may use at most 192 MiB of HBM per device.

```python
import math
import jax
import jax.numpy as jnp
from jax import lax

B = 64
KL = 30
KS = 20
KC = 24
HL = 15
SW = 7
CW = 16
NB = 2048
KSP = 5
KCP = 6


def pick_distinct(key, count, span, keep):
    scores = jax.random.randint(key, (count, span), 0, 1 << 20) * span + jnp.arange(span, dtype=jnp.int32)[None, :]
    order = jnp.argsort(scores, axis=1)
    return jnp.sort(order[:, :keep], axis=1).astype(jnp.int32)


def partition_cols(key, keep, span, nparts):
    per_part = NB // nparts
    positions = jnp.arange(NB, dtype=jnp.int32)
    start = jnp.clip(positions // nparts - span // 2, 0, per_part - span)
    pieces = []
    for part_id in range(nparts):
        chosen = pick_distinct(jax.random.fold_in(key, part_id + 11), NB, span, keep)
        pieces.append(nparts * (start[:, None] + chosen) + part_id)
    return jnp.concatenate(pieces, axis=1).astype(jnp.int32)


def draw_l_index(key, part):
    span = 2 * HL + 1
    positions = jnp.arange(NB, dtype=jnp.int32)
    start = jnp.clip(positions - HL, 0, NB - span)
    return (start[:, None] + pick_distinct(jax.random.fold_in(key, 3), NB, span, KL)).astype(jnp.int32)


def draw_s_cols(key, part):
    return partition_cols(jax.random.fold_in(key, 5), KSP, SW, KS // KSP)


def draw_c_index(key, part):
    return partition_cols(jax.random.fold_in(key, 7), KCP, CW, KC // KCP)


def block_levels(key, extent, cuts, least, largest):
    factor_of = 1.0
    for dim, blocks in cuts:
        steps = jax.random.uniform(jax.random.fold_in(jax.random.fold_in(key, 6), dim), (blocks,), jnp.float32, least / len(cuts), largest / len(cuts))
        factor_of = factor_of * jnp.repeat(jnp.exp(steps), extent[dim] // blocks).reshape((-1,) + (1,) * (len(extent) - 1 - dim))
    return factor_of


def bell_draw(key, shape, spread, most, cuts=(), kind=jnp.bfloat16):
    entries = spread * jax.random.normal(key, shape, jnp.float32)
    if cuts:
        entries = entries * block_levels(key, shape, cuts, -0.22, 0.18)
    return jnp.clip(entries, -most, most).astype(kind)


def setup_inputs(seed: int = 0) -> dict:
    arg_keys = jax.random.split(jax.random.key(seed), 6)
    l_blocks = bell_draw(arg_keys[0], (NB, B, KL * B), (9 * B) ** -0.5, 0.25, ((0, 256),))
    s_blocks = bell_draw(arg_keys[1], (NB, B, KS * B), 1.0, 6.0, ((0, 64), (2, 4)))
    l_index = draw_l_index(jax.random.fold_in(arg_keys[5], 71), 0)
    s_cols = draw_s_cols(jax.random.fold_in(arg_keys[5], 71), 0)
    c_index = draw_c_index(jax.random.fold_in(arg_keys[5], 71), 0)
    return dict(l_blocks=l_blocks, s_blocks=s_blocks, l_index=l_index, s_cols=s_cols, c_index=c_index)


def block_row(left_row, left_ids, want_cols, s_four, s_cols):
    width = s_four.shape[1]
    slot_total = s_four.shape[2]
    slot_ids = jnp.take(s_cols, left_ids, axis=0)
    match = slot_ids[:, None, :] == want_cols[None, :, None]
    slot_pick = jnp.sum(jnp.where(match, lax.iota(jnp.int32, slot_total)[None, None, :], 0), axis=2, dtype=jnp.int32)
    found = jnp.any(match, axis=2)
    picked = s_four[left_ids.astype(jnp.int32)[:, None], :, slot_pick, :]
    picked = jnp.where(found[:, :, None, None], picked.astype(jnp.float32), jnp.float32(0.0))
    left_three = left_row.reshape(width, left_ids.shape[0], width).astype(jnp.float32)
    summed = jnp.einsum('akb,kmbc->amc', left_three, picked, precision=lax.Precision.HIGHEST)
    return summed.reshape(width, want_cols.shape[0] * width).astype(jnp.bfloat16)


def reference(l_blocks, s_blocks, l_index, s_cols, c_index):
    total = l_blocks.shape[0]
    width = l_blocks.shape[1]
    s_four = s_blocks.reshape(total, width, s_blocks.shape[2] // width, width)
    per_turn = math.gcd(total, 8)

    def single(left_row, left_ids, want_cols):
        return block_row(left_row, left_ids, want_cols, s_four, s_cols)

    def one_group(group):
        return jax.vmap(single)(group[0], group[1], group[2])

    shaped = tuple(a.reshape((total // per_turn, per_turn) + a.shape[1:]) for a in (l_blocks, l_index, c_index))
    result = lax.map(one_group, shaped)
    return result.reshape((total,) + result.shape[2:])
```

```python
import functools

import jax
import jax.numpy as jnp
from jax import lax
from jax.experimental import pallas as pl
from jax.experimental.pallas import tpu as pltpu
from jax.sharding import PartitionSpec as P

HALF = 16
TILES = 40
ZERO = 6 * TILES


def pack_body(start_ref, s_ref, first_ref, second_ref):
    def one(out_ref, base):
        def row(j, carry):
            for t in range(2):
                out_ref[2 * j + t] = s_ref[base + j, :, 128 * t : 128 * t + 128]
            return carry

        lax.fori_loop(0, HALF, row, 0, unroll=4)

        def pair(j, carry):
            out_ref[32 + j] = jnp.concatenate(
                [s_ref[base + 2 * j, :, 256:320], s_ref[base + 2 * j + 1, :, 256:320]], axis=1
            )
            return carry

        lax.fori_loop(0, HALF // 2, pair, 0, unroll=4)

    h = start_ref[0]
    one(first_ref, HALF * h)
    one(second_ref, HALF * (1 - h))


def pack(h, s_blocks):
    piece = jax.ShapeDtypeStruct((TILES, 64, 128), jnp.bfloat16)
    return pl.pallas_call(
        pack_body,
        out_shape=(piece, piece),
        in_specs=[
            pl.BlockSpec(memory_space=pltpu.SMEM),
            pl.BlockSpec(memory_space=pltpu.VMEM),
        ],
        out_specs=(
            pl.BlockSpec(memory_space=pltpu.VMEM),
            pl.BlockSpec(memory_space=pltpu.VMEM),
        ),
        compiler_params=pltpu.CompilerParams(vmem_limit_bytes=16 << 20),
        cost_estimate=pl.CostEstimate(flops=0, bytes_accessed=3 << 20, transcendentals=0),
    )(h, s_blocks)


def product_body(tab_ref, part_ref, l_ref, a_ref, b_ref, c_ref, *rest):
    o_ref, sd_ref, pk_ref = rest[-3:]
    i = pl.program_id(0)

    @pl.when(i == 0)
    def _():
        for n, piece in enumerate((a_ref, b_ref, c_ref)):

            def spread(t, carry, piece=piece, n=n):
                v = piece[t]
                lo, hi = v[:, :64], v[:, 64:]
                sd_ref[2 * TILES * n + 2 * t] = jnp.concatenate([lo, lo], axis=1)
                sd_ref[2 * TILES * n + 2 * t + 1] = jnp.concatenate([hi, hi], axis=1)
                return carry

            lax.fori_loop(0, TILES, spread, 0, unroll=4)
        sd_ref[ZERO] = jnp.zeros((64, 128), jnp.bfloat16)

    base = part_ref[0] * 6
    low = lax.broadcasted_iota(jnp.int32, (64, 128), 1) < 64

    def lay(k, carry):
        row = i * 30 + k
        for m in range(3):
            x = sd_ref[tab_ref[row, base + 2 * m]]
            y = sd_ref[tab_ref[row, base + 2 * m + 1]]
            pk_ref[pl.ds(k * 64, 64), 128 * m : 128 * m + 128] = jnp.where(low, x, y)
        return carry

    lax.fori_loop(0, 30, lay, 0, unroll=6)
    o_ref[0] = jnp.dot(
        l_ref[0], pk_ref[...], preferred_element_type=jnp.float32
    ).astype(o_ref.dtype)


def product(tab, part, l_blocks, pieces, prev):
    rows = l_blocks.shape[0]
    whole = pl.BlockSpec((TILES, 64, 128), lambda i, t, p: (0, 0, 0), pipeline_mode=pl.Buffered(1))
    in_specs = [pl.BlockSpec((1, 64, 1920), lambda i, t, p: (i, 0, 0)), whole, whole, whole]
    args = [tab, part, l_blocks, *pieces]
    aliases = {}
    if prev is not None:
        in_specs.append(pl.BlockSpec(memory_space=pl.ANY))
        aliases = {len(args): 0}
        args.append(prev)
    return pl.pallas_call(
        product_body,
        out_shape=jax.ShapeDtypeStruct((rows, 64, 1536), jnp.bfloat16),
        grid_spec=pltpu.PrefetchScalarGridSpec(
            num_scalar_prefetch=2,
            grid=(rows,),
            in_specs=in_specs,
            out_specs=pl.BlockSpec((1, 64, 384), lambda i, t, p: (i, 0, p[0])),
            scratch_shapes=[
                pltpu.VMEM((ZERO + 1, 64, 128), jnp.bfloat16),
                pltpu.VMEM((1920, 384), jnp.bfloat16),
            ],
        ),
        input_output_aliases=aliases,
        compiler_params=pltpu.CompilerParams(vmem_limit_bytes=24 << 20),
        cost_estimate=pl.CostEstimate(flops=755_000_000, bytes_accessed=4 << 20, transcendentals=0),
    )(*args)


def table(h, r, l_index, s_cols, c_index):
    total = s_cols.shape[0]
    rows, terms = l_index.shape
    kept = c_index.shape[1]
    near = 4 * HALF
    w0 = jnp.clip(32 * r - HALF, 0, total - near)
    window = lax.dynamic_slice_in_dim(s_cols, w0, near, axis=0).astype(jnp.float32)
    lane = lax.broadcasted_iota(jnp.int32, (20, 5 * kept), 1)
    source = (lane % kept) // 6 * 5 + lane // kept
    spread = (source == lax.broadcasted_iota(jnp.int32, (20, 5 * kept), 0)).astype(jnp.float32)
    slots = jnp.dot(window, spread, precision=lax.Precision.HIGHEST)
    flat = l_index.reshape(rows * terms, 1)
    hot = (flat - w0 == lax.broadcasted_iota(jnp.int32, (rows * terms, near), 1)).astype(jnp.float32)
    cols = jnp.dot(hot, slots, precision=lax.Precision.HIGHEST)
    want = jnp.broadcast_to(c_index[:, None, :], (rows, terms, kept)).reshape(rows * terms, kept)
    want = want.astype(jnp.float32)
    d = flat - 32 * r
    part = lax.broadcasted_iota(jnp.int32, (rows * terms, kept), 1) // 6
    remote = (part // 2 != h).astype(jnp.int32)
    inside = (d >= 0) & (d < 32)
    piece = jnp.where(inside, (d // HALF) ^ h ^ remote, 2)
    j = d & (HALF - 1)
    where = jnp.full((rows * terms, kept), ZERO, jnp.int32)
    for s in range(5):
        place = piece * (2 * TILES) + (4 * j + s if s < 4 else 64 + j)
        where = jnp.where(cols[:, s * kept : (s + 1) * kept] == want, place, where)
    return where


def shards(l_blocks, s_blocks, l_index, s_cols, c_index):
    r, c = lax.axis_index("rows"), lax.axis_index("cols")
    groups = lax.axis_size("rows")
    h = c // 2
    across = functools.partial(lax.ppermute, axis_name="cols", perm=[(k, k ^ 2) for k in range(4)])
    beside = functools.partial(lax.ppermute, axis_name="cols", perm=[(k, k ^ 1) for k in range(4)])
    up = [(4 * g + k, 4 * g + 4 + k) for g in range(groups - 1) for k in (0, 1)]
    down = [(4 * g + k, 4 * g - 4 + k) for g in range(1, groups) for k in (2, 3)]
    along = functools.partial(lax.ppermute, axis_name=("rows", "cols"), perm=up + down)

    first, second = pack(h.reshape(1), s_blocks)
    far_first = across(first)
    halo = along(second)
    far_second = across(second)
    mate_first, mate_second = beside(first), beside(second)
    far_halo = along(far_first)
    mate_halo = beside(halo)
    cross_first = beside(far_first)
    cross_second = beside(far_second)
    cross_halo = beside(far_halo)

    tab = table(h, r, l_index, s_cols, c_index)
    out = None
    for flip, pieces in (
        (0, (first, second, halo)),
        (1, (mate_first, mate_second, mate_halo)),
        (2, (far_first, far_second, far_halo)),
        (3, (cross_first, cross_second, cross_halo)),
    ):
        out = product(tab, (c ^ flip).reshape(1), l_blocks, pieces, out)
    return out


def solution(mesh):
    return jax.shard_map(
        shards,
        mesh=mesh,
        in_specs=(
            P(("rows", "cols"), None, None),
            P("rows", None, "cols"),
            P(("rows", "cols"), None),
            P(),
            P(("rows", "cols"), None),
        ),
        out_specs=P(("rows", "cols"), None, None),
        check_vma=False,
    )
```

```python
import functools

import jax
import jax.numpy as jnp
from jax import lax
from jax.experimental import pallas as pl
from jax.experimental.pallas import tpu as pltpu
from jax.sharding import PartitionSpec as P

HALF = 16
TILES = 40
ZERO = 6 * TILES


def pack_body(start_ref, s_ref, first_ref, second_ref, both_ref):
    def row(j, carry):
        for out_ref, base in places:
            for t in range(2):
                out_ref[2 * j + t] = s_ref[base + j, :, 128 * t : 128 * t + 128]
        return carry

    def pair(j, carry):
        for out_ref, base in places:
            out_ref[32 + j] = jnp.concatenate(
                [s_ref[base + 2 * j, :, 256:320], s_ref[base + 2 * j + 1, :, 256:320]], axis=1
            )
        return carry

    places = ((first_ref, HALF * start_ref[0]), (second_ref, HALF * (1 - start_ref[0])))
    lax.fori_loop(0, HALF, row, 0, unroll=4)
    lax.fori_loop(0, HALF // 2, pair, 0, unroll=4)
    both_ref[:TILES] = first_ref[...]
    both_ref[TILES:] = second_ref[...]


def pack(start, s_blocks):
    piece = jax.ShapeDtypeStruct((TILES, 64, 128), jnp.bfloat16)
    both = jax.ShapeDtypeStruct((2 * TILES, 64, 128), jnp.bfloat16)
    vmem = pl.BlockSpec(memory_space=pltpu.VMEM)
    return pl.pallas_call(
        pack_body,
        out_shape=(piece, piece, both),
        in_specs=[pl.BlockSpec(memory_space=pltpu.SMEM), vmem],
        out_specs=(vmem,) * 3,
        compiler_params=pltpu.CompilerParams(vmem_limit_bytes=16 << 20),
        cost_estimate=pl.CostEstimate(flops=0, bytes_accessed=3 << 20, transcendentals=0),
    )(start, s_blocks)


def product_body(count, tab_ref, part_ref, l_ref, *rest):
    o_ref, sd_ref, ob_ref, sem = rest[-4:]
    rows = l_ref.shape[0]
    base = 0
    for piece in rest[:count]:

        def spread(t, carry, piece=piece, base=base):
            v = piece[t]
            sd_ref[base + 2 * t] = v
            sd_ref[base + 2 * t + 1] = jnp.concatenate([v[:, 64:], v[:, :64]], axis=1)
            return carry

        lax.fori_loop(0, piece.shape[0], spread, 0, unroll=8)
        base += 2 * piece.shape[0]
    for zero in (ZERO, ZERO + 1):
        sd_ref[zero] = jnp.zeros((64, 128), jnp.bfloat16)
    part = part_ref[0]
    low = lax.broadcasted_iota(jnp.int32, (64, 128), 1) < 64

    def out(i):
        lanes = pl.ds(pl.multiple_of(part * 384, 128), 384)
        return pltpu.make_async_copy(ob_ref.at[i], o_ref.at[i, :, lanes], sem.at[i])

    def row(i, carry):
        def pick(k, m):
            at = (i * 30 + k) * 24 + part * 6 + 2 * m
            return jnp.where(low, sd_ref[tab_ref[at]], sd_ref[tab_ref[at + 1]])

        total = jnp.zeros((64, 384), jnp.float32)
        for k0 in range(0, 30, 4):
            ks = range(k0, min(k0 + 4, 30))
            picked = jnp.concatenate(
                [jnp.concatenate([pick(k, m) for m in range(3)], axis=1) for k in ks], axis=0
            )
            total = total + jnp.dot(
                l_ref[i, :, 64 * k0 : 64 * (k0 + len(ks))], picked, preferred_element_type=jnp.float32
            )
        ob_ref[i] = total.astype(o_ref.dtype)
        out(i).start()
        return carry

    lax.fori_loop(0, rows, row, 0)

    def finish(i, carry):
        out(i).wait()
        return carry

    lax.fori_loop(0, rows, finish, 0)


def product(tab, part, l_blocks, pieces, prev):
    rows = l_blocks.shape[0]
    vmem, smem = pl.BlockSpec(memory_space=pltpu.VMEM), pl.BlockSpec(memory_space=pltpu.SMEM)
    in_specs = [smem, smem] + [vmem] * (1 + len(pieces))
    args = [tab, part, l_blocks, *pieces]
    aliases = {}
    if prev is not None:
        in_specs.append(pl.BlockSpec(memory_space=pl.ANY))
        aliases = {len(args): 0}
        args.append(prev)
    return pl.pallas_call(
        functools.partial(product_body, len(pieces)),
        out_shape=jax.ShapeDtypeStruct((rows, 64, 1536), jnp.bfloat16),
        in_specs=in_specs,
        out_specs=pl.BlockSpec(memory_space=pl.ANY),
        scratch_shapes=[
            pltpu.VMEM((ZERO + 2, 64, 128), jnp.bfloat16),
            pltpu.VMEM((rows, 64, 384), jnp.bfloat16),
            pltpu.SemaphoreType.DMA((rows,)),
        ],
        input_output_aliases=aliases,
        compiler_params=pltpu.CompilerParams(vmem_limit_bytes=24 << 20),
        cost_estimate=pl.CostEstimate(flops=755_000_000, bytes_accessed=20 << 20, transcendentals=0),
    )(*args)


def table(h, r, l_index, s_cols, c_index):
    total = s_cols.shape[0]
    rows, terms = l_index.shape
    kept = c_index.shape[1]
    near = 4 * HALF
    w0 = jnp.clip(32 * r - HALF, 0, total - near)
    window = lax.dynamic_slice_in_dim(s_cols, w0, near, axis=0).astype(jnp.float32)
    lane = lax.broadcasted_iota(jnp.int32, (20, 5 * kept), 1)
    source = (lane % kept) // 6 * 5 + lane // kept
    spread = (source == lax.broadcasted_iota(jnp.int32, (20, 5 * kept), 0)).astype(jnp.float32)
    slots = jnp.dot(window, spread, precision=lax.Precision.HIGHEST)
    flat = l_index.reshape(rows * terms, 1)
    hot = (flat - w0 == lax.broadcasted_iota(jnp.int32, (rows * terms, near), 1)).astype(jnp.float32)
    cols = jnp.dot(hot, slots, precision=lax.Precision.HIGHEST)
    want = jnp.broadcast_to(c_index[:, None, :], (rows, terms, kept)).reshape(rows * terms, kept)
    want = want.astype(jnp.float32)
    d = flat - 32 * r
    part = lax.broadcasted_iota(jnp.int32, (rows * terms, kept), 1) // 6
    remote = (part // 2 != h).astype(jnp.int32)
    inside = (d >= 0) & (d < 32)
    piece = jnp.where(inside, (d // HALF) ^ h ^ remote, 2)
    j = d & (HALF - 1)
    where = jnp.full((rows * terms, kept), ZERO, jnp.int32)
    odd = lax.broadcasted_iota(jnp.int32, (rows * terms, kept), 1) & 1
    for s in range(5):
        place = piece * (2 * TILES) + (4 * j + s if s < 4 else 64 + j)
        where = jnp.where(cols[:, s * kept : (s + 1) * kept] == want, place, where)
    return (where ^ odd).reshape(rows * terms * kept)


def shards(l_blocks, s_blocks, l_index, s_cols, c_index):
    r, c = lax.axis_index("rows"), lax.axis_index("cols")
    groups = lax.axis_size("rows")
    h = c // 2
    across = functools.partial(lax.ppermute, axis_name="cols", perm=[(k, k ^ 2) for k in range(4)])
    beside = functools.partial(lax.ppermute, axis_name="cols", perm=[(k, k ^ 1) for k in range(4)])
    up = [(4 * g + k, 4 * g + 4 + k) for g in range(groups - 1) for k in (0, 1)]
    down = [(4 * g + k, 4 * g - 4 + k) for g in range(1, groups) for k in (2, 3)]
    below, above = groups // 2 - 1, groups // 2
    seam = [(4 * below + 2 + k, 4 * above + k) for k in (0, 1)]
    seam += [(4 * above + k, 4 * below + 2 + k) for k in (0, 1)]
    plain = [route for route in up + down if route[1] not in {q for _, q in seam}]
    takes = ((r == above) & (h == 0)) | ((r == below) & (h == 1))

    def send(x, perm):
        return lax.ppermute(x, ("rows", "cols"), perm)

    first, second, both = pack(h.reshape(1), s_blocks)
    far_first = across(first)
    halo = send(second, up + down)
    seam_halo = send(first, seam)
    tab = table(h, r, l_index, s_cols, c_index)
    second, both, tab = lax.optimization_barrier((second, both, tab))
    far_second = across(second)
    mate = beside(both)

    far_halo = send(far_first, plain)
    cross_first = beside(far_first)
    mate_halo = beside(halo)
    tab, far_first = lax.optimization_barrier((tab, far_first))
    parts = [(c ^ flip).reshape(1) for flip in range(4)]
    out = product(tab, parts[0], l_blocks, (both, halo), None)
    out = product(tab, parts[1], l_blocks, (mate, mate_halo), out)
    out, far_second, far_halo = lax.optimization_barrier((out, far_second, far_halo))
    cross_second = beside(far_second)
    far_halo = jnp.where(takes, seam_halo, far_halo)
    cross_halo = beside(far_halo)
    out = product(tab, parts[2], l_blocks, (far_first, far_second, far_halo), out)
    return product(tab, parts[3], l_blocks, (cross_first, cross_second, cross_halo), out)


def solution(mesh):
    return jax.shard_map(
        shards,
        mesh=mesh,
        in_specs=(
            P(("rows", "cols"), None, None),
            P("rows", None, "cols"),
            P(("rows", "cols"), None),
            P(),
            P(("rows", "cols"), None),
        ),
        out_specs=P(("rows", "cols"), None, None),
        check_vma=False,
    )
```

```python
import functools

import jax
import jax.numpy as jnp
from jax import lax
from jax.experimental import pallas as pl
from jax.experimental.pallas import tpu as pltpu
from jax.sharding import PartitionSpec as P

HALF = 16
TILES = 40
RAW = 6 * 2 * HALF
ZERO = RAW + 2 * TILES


def pack_body(start_ref, s_ref, first_ref, second_ref):
    def row(j, carry):
        for out_ref, base in places:
            for t in range(2):
                out_ref[2 * j + t] = s_ref[base + j, :, 128 * t : 128 * t + 128]
        return carry

    def pair(j, carry):
        for out_ref, base in places:
            out_ref[32 + j] = jnp.concatenate(
                [s_ref[base + 2 * j, :, 256:320], s_ref[base + 2 * j + 1, :, 256:320]], axis=1
            )
        return carry

    places = ((first_ref, HALF * start_ref[0]), (second_ref, HALF * (1 - start_ref[0])))
    lax.fori_loop(0, HALF, row, 0, unroll=4)
    lax.fori_loop(0, HALF // 2, pair, 0, unroll=4)


def pack(start, s_blocks):
    piece = jax.ShapeDtypeStruct((TILES, 64, 128), jnp.bfloat16)
    vmem = pl.BlockSpec(memory_space=pltpu.VMEM)
    return pl.pallas_call(
        pack_body,
        out_shape=(piece, piece),
        in_specs=[pl.BlockSpec(memory_space=pltpu.SMEM), vmem],
        out_specs=(vmem,) * 2,
        compiler_params=pltpu.CompilerParams(vmem_limit_bytes=16 << 20),
        cost_estimate=pl.CostEstimate(flops=0, bytes_accessed=3 << 20, transcendentals=0),
    )(start, s_blocks)


def product_body(count, tab_ref, part_ref, l_ref, *rest):
    o_ref, sd_ref, ob_ref, sem = rest[-4:]
    rows = l_ref.shape[0]
    base = 0
    for piece in rest[:count]:
        packed = piece.shape[2] == 128

        def spread(t, carry, piece=piece, base=base, packed=packed):
            for u in range(1 if packed else 2):
                v = piece[t, :, 128 * u : 128 * u + 128]
                at = base + 2 * t if packed else base + 6 * t + 2 * u
                sd_ref[at] = v
                sd_ref[at + 1] = jnp.concatenate([v[:, 64:], v[:, :64]], axis=1)
            if not packed:
                v = piece[t, :, 256:320]
                v = jnp.concatenate([v, v], axis=1)
                sd_ref[base + 6 * t + 4] = v
                sd_ref[base + 6 * t + 5] = v
            return carry

        lax.fori_loop(0, piece.shape[0], spread, 0, unroll=8 if packed else 4)
        base += 2 * TILES if packed else RAW
    for zero in (ZERO, ZERO + 1):
        sd_ref[zero] = jnp.zeros((64, 128), jnp.bfloat16)
    part = part_ref[0]
    low = lax.broadcasted_iota(jnp.int32, (64, 128), 1) < 64

    def out(i):
        lanes = pl.ds(pl.multiple_of(part * 384, 128), 384)
        return pltpu.make_async_copy(ob_ref.at[i], o_ref.at[i, :, lanes], sem.at[i])

    def row(i, carry):
        def pick(k, m):
            at = (i * 30 + k) * 24 + part * 6 + 2 * m
            return jnp.where(low, sd_ref[tab_ref[at]], sd_ref[tab_ref[at + 1]])

        total = jnp.zeros((64, 384), jnp.float32)
        for k0 in range(0, 30, 4):
            ks = range(k0, min(k0 + 4, 30))
            picked = jnp.concatenate(
                [jnp.concatenate([pick(k, m) for m in range(3)], axis=1) for k in ks], axis=0
            )
            total = total + jnp.dot(
                l_ref[i, :, 64 * k0 : 64 * (k0 + len(ks))], picked, preferred_element_type=jnp.float32
            )
        ob_ref[i] = total.astype(o_ref.dtype)
        out(i).start()
        return carry

    lax.fori_loop(0, rows, row, 0, unroll=True)

    def finish(i, carry):
        out(i).wait()
        return carry

    lax.fori_loop(0, rows, finish, 0)


def product(tab, part, l_blocks, pieces, prev):
    rows = l_blocks.shape[0]
    vmem, smem = pl.BlockSpec(memory_space=pltpu.VMEM), pl.BlockSpec(memory_space=pltpu.SMEM)
    in_specs = [smem, smem] + [vmem] * (1 + len(pieces))
    args = [tab, part, l_blocks, *pieces]
    aliases = {}
    if prev is not None:
        in_specs.append(pl.BlockSpec(memory_space=pl.ANY))
        aliases = {len(args): 0}
        args.append(prev)
    return pl.pallas_call(
        functools.partial(product_body, len(pieces)),
        out_shape=jax.ShapeDtypeStruct((rows, 64, 1536), jnp.bfloat16),
        in_specs=in_specs,
        out_specs=pl.BlockSpec(memory_space=pl.ANY),
        scratch_shapes=[
            pltpu.VMEM((ZERO + 2, 64, 128), jnp.bfloat16),
            pltpu.VMEM((rows, 64, 384), jnp.bfloat16),
            pltpu.SemaphoreType.DMA((rows,)),
        ],
        input_output_aliases=aliases,
        compiler_params=pltpu.CompilerParams(vmem_limit_bytes=24 << 20),
        cost_estimate=pl.CostEstimate(flops=755_000_000, bytes_accessed=20 << 20, transcendentals=0),
    )(*args)


def table(h, r, l_index, s_cols, c_index):
    total = s_cols.shape[0]
    rows, terms = l_index.shape
    kept = c_index.shape[1]
    near = 4 * HALF
    w0 = jnp.clip(32 * r - HALF, 0, total - near)
    window = lax.dynamic_slice_in_dim(s_cols, w0, near, axis=0).astype(jnp.float32)
    lane = lax.broadcasted_iota(jnp.int32, (20, 5 * kept), 1)
    source = (lane % kept) // 6 * 5 + lane // kept
    spread = (source == lax.broadcasted_iota(jnp.int32, (20, 5 * kept), 0)).astype(jnp.float32)
    slots = jnp.dot(window, spread, precision=lax.Precision.HIGHEST)
    flat = l_index.reshape(rows * terms, 1)
    hot = (flat - w0 == lax.broadcasted_iota(jnp.int32, (rows * terms, near), 1)).astype(jnp.float32)
    cols = jnp.dot(hot, slots, precision=lax.Precision.HIGHEST)
    want = jnp.broadcast_to(c_index[:, None, :], (rows, terms, kept)).reshape(rows * terms, kept)
    want = want.astype(jnp.float32)
    d = flat - 32 * r
    part = lax.broadcasted_iota(jnp.int32, (rows * terms, kept), 1) // 6
    remote = part // 2 != h
    inside = (d >= 0) & (d < 32)
    piece = jnp.where(inside, (d // HALF) ^ h ^ 1, 2) * (2 * TILES)
    j = d & (HALF - 1)
    odd = lax.broadcasted_iota(jnp.int32, (rows * terms, kept), 1) & 1
    where = jnp.full((rows * terms, kept), ZERO, jnp.int32)
    for s in range(5):
        near_place = jnp.where(inside, 6 * d + s, RAW + (4 * j + s if s < 4 else 64 + j))
        far_place = piece + (4 * j + s if s < 4 else 64 + j)
        place = jnp.where(remote, far_place, near_place)
        where = jnp.where(cols[:, s * kept : (s + 1) * kept] == want, place, where)
    return (where ^ odd).reshape(rows * terms * kept)


def shards(l_blocks, s_blocks, l_index, s_cols, c_index):
    r, c = lax.axis_index("rows"), lax.axis_index("cols")
    groups = lax.axis_size("rows")
    h = c // 2
    across = functools.partial(lax.ppermute, axis_name="cols", perm=[(k, k ^ 2) for k in range(4)])
    beside = functools.partial(lax.ppermute, axis_name="cols", perm=[(k, k ^ 1) for k in range(4)])
    up = [(4 * g + k, 4 * g + 4 + k) for g in range(groups - 1) for k in (0, 1)]
    down = [(4 * g + k, 4 * g - 4 + k) for g in range(1, groups) for k in (2, 3)]
    below, above = groups // 2 - 1, groups // 2
    seam = [(4 * below + 2 + k, 4 * above + k) for k in (0, 1)]
    seam += [(4 * above + k, 4 * below + 2 + k) for k in (0, 1)]
    plain = [route for route in up + down if route[1] not in {q for _, q in seam}]
    takes = ((r == above) & (h == 0)) | ((r == below) & (h == 1))

    def send(x, perm):
        return lax.ppermute(x, ("rows", "cols"), perm)

    first, second = pack(h.reshape(1), s_blocks)
    far_first = across(first)
    halo = send(second, up + down)
    seam_halo = send(first, seam)
    mate, first = lax.optimization_barrier((s_blocks, first))
    mate = beside(mate)
    tab = table(h, r, l_index, s_cols, c_index)
    second, tab = lax.optimization_barrier((second, tab))
    far_second = across(second)

    far_halo = send(far_first, plain)
    cross_first = beside(far_first)
    mate_halo = beside(halo)
    tab, far_first = lax.optimization_barrier((tab, far_first))
    parts = [(c ^ flip).reshape(1) for flip in range(4)]
    out = product(tab, parts[0], l_blocks, (s_blocks, halo), None)
    out = product(tab, parts[1], l_blocks, (mate, mate_halo), out)
    out, far_second, far_halo = lax.optimization_barrier((out, far_second, far_halo))
    cross_second = beside(far_second)
    far_halo = jnp.where(takes, seam_halo, far_halo)
    cross_halo = beside(far_halo)
    out = product(tab, parts[2], l_blocks, (far_first, far_second, far_halo), out)
    return product(tab, parts[3], l_blocks, (cross_first, cross_second, cross_halo), out)


def solution(mesh):
    return jax.shard_map(
        shards,
        mesh=mesh,
        in_specs=(
            P(("rows", "cols"), None, None),
            P("rows", None, "cols"),
            P(("rows", "cols"), None),
            P(),
            P(("rows", "cols"), None),
        ),
        out_specs=P(("rows", "cols"), None, None),
        check_vma=False,
    )
```

```python
import functools

import jax
import jax.numpy as jnp
from jax import lax
from jax.experimental import pallas as pl
from jax.experimental.pallas import tpu as pltpu
from jax.sharding import PartitionSpec as P

HALF = 16
TILES = 40
RAW = 6 * 2 * HALF
ZERO = RAW + 2 * TILES


def pack_body(start_ref, s_ref, first_ref, second_ref):
    def row(j, carry):
        for out_ref, base in places:
            for t in range(2):
                out_ref[2 * j + t] = s_ref[base + j, :, 128 * t : 128 * t + 128]
        return carry

    def pair(j, carry):
        for out_ref, base in places:
            out_ref[32 + j] = jnp.concatenate(
                [s_ref[base + 2 * j, :, 256:320], s_ref[base + 2 * j + 1, :, 256:320]], axis=1
            )
        return carry

    places = ((first_ref, HALF * start_ref[0]), (second_ref, HALF * (1 - start_ref[0])))
    lax.fori_loop(0, HALF, row, 0, unroll=4)
    lax.fori_loop(0, HALF // 2, pair, 0, unroll=4)


def pack(start, s_blocks):
    piece = jax.ShapeDtypeStruct((TILES, 64, 128), jnp.bfloat16)
    vmem = pl.BlockSpec(memory_space=pltpu.VMEM)
    return pl.pallas_call(
        pack_body,
        out_shape=(piece, piece),
        in_specs=[pl.BlockSpec(memory_space=pltpu.SMEM), vmem],
        out_specs=(vmem,) * 2,
        compiler_params=pltpu.CompilerParams(vmem_limit_bytes=16 << 20),
        cost_estimate=pl.CostEstimate(flops=0, bytes_accessed=3 << 20, transcendentals=0),
    )(start, s_blocks)


def product_body(count, tab_ref, part_ref, l_ref, *rest):
    o_ref, sd_ref, ob_ref, sem = rest[-4:]
    rows = l_ref.shape[0]
    base = 0
    for piece in rest[:count]:
        packed = piece.shape[2] == 128

        def spread(t, carry, piece=piece, base=base, packed=packed):
            for u in range(1 if packed else 2):
                v = piece[t, :, 128 * u : 128 * u + 128]
                at = base + 2 * t if packed else base + 6 * t + 2 * u
                sd_ref[at] = v
                sd_ref[at + 1] = jnp.concatenate([v[:, 64:], v[:, :64]], axis=1)
            if not packed:
                v = piece[t, :, 256:320]
                v = jnp.concatenate([v, v], axis=1)
                sd_ref[base + 6 * t + 4] = v
                sd_ref[base + 6 * t + 5] = v
            return carry

        lax.fori_loop(0, piece.shape[0], spread, 0, unroll=8 if packed else 4)
        base += 2 * TILES if packed else RAW
    for zero in (ZERO, ZERO + 1):
        sd_ref[zero] = jnp.zeros((64, 128), jnp.bfloat16)
    part = part_ref[0]
    low = lax.broadcasted_iota(jnp.int32, (64, 128), 1) < 64

    def out(i):
        lanes = pl.ds(pl.multiple_of(part * 384, 128), 384)
        return pltpu.make_async_copy(ob_ref.at[i], o_ref.at[i, :, lanes], sem.at[i])

    def row(i, carry):
        def pick(k, m):
            at = (k // 5 * 8 + i) * 128 + k % 5 * 24 + part * 6 + 2 * m
            return jnp.where(low, sd_ref[tab_ref[at]], sd_ref[tab_ref[at + 1]])

        total = jnp.zeros((64, 384), jnp.float32)
        for k0 in range(0, 30, 4):
            ks = range(k0, min(k0 + 4, 30))
            picked = jnp.concatenate(
                [jnp.concatenate([pick(k, m) for m in range(3)], axis=1) for k in ks], axis=0
            )
            total = total + jnp.dot(
                l_ref[i, :, 64 * k0 : 64 * (k0 + len(ks))], picked, preferred_element_type=jnp.float32
            )
        ob_ref[i] = total.astype(o_ref.dtype)
        out(i).start()
        return carry

    lax.fori_loop(0, rows, row, 0, unroll=True)

    def finish(i, carry):
        out(i).wait()
        return carry

    lax.fori_loop(0, rows, finish, 0)


def product(tab, part, l_blocks, pieces, prev):
    rows = l_blocks.shape[0]
    vmem, smem = pl.BlockSpec(memory_space=pltpu.VMEM), pl.BlockSpec(memory_space=pltpu.SMEM)
    in_specs = [smem, smem] + [vmem] * (1 + len(pieces))
    args = [tab, part, l_blocks, *pieces]
    aliases = {}
    if prev is not None:
        in_specs.append(pl.BlockSpec(memory_space=pl.ANY))
        aliases = {len(args): 0}
        args.append(prev)
    return pl.pallas_call(
        functools.partial(product_body, len(pieces)),
        out_shape=jax.ShapeDtypeStruct((rows, 64, 1536), jnp.bfloat16),
        in_specs=in_specs,
        out_specs=pl.BlockSpec(memory_space=pl.ANY),
        scratch_shapes=[
            pltpu.VMEM((ZERO + 2, 64, 128), jnp.bfloat16),
            pltpu.VMEM((rows, 64, 384), jnp.bfloat16),
            pltpu.SemaphoreType.DMA((rows,)),
        ],
        input_output_aliases=aliases,
        compiler_params=pltpu.CompilerParams(vmem_limit_bytes=24 << 20),
        cost_estimate=pl.CostEstimate(flops=755_000_000, bytes_accessed=20 << 20, transcendentals=0),
    )(*args)


def split(v):
    return [x.astype(jnp.float32).astype(jnp.bfloat16) for x in (v >> 6, v & 63)]


def exact(a, b, dims):
    return lax.dot_general(a, b, (dims, ((), ())), preferred_element_type=jnp.float32)


def table_body(at_ref, near_ref, l_ref, c_ref, tab_ref):
    start, first, h = at_ref[0], at_ref[1], at_ref[2]

    def places(shape, dim):
        lane = lax.broadcasted_iota(jnp.int32, shape, dim)
        k = sum((lane >= 24 * t).astype(jnp.int32) for t in range(1, 5))
        m = lane - 24 * k
        return k, m, sum((m >= 6 * t).astype(jnp.int32) for t in range(1, 4))

    k_of, m_of, part = places((48, 128), 1)
    _, m_wide, _ = places((24, 128), 1)
    tile = (lax.broadcasted_iota(jnp.int32, (24, 128), 0) == m_wide).astype(jnp.float32).astype(jnp.bfloat16)
    want = [exact(x, tile, ((1,), (0,))) for x in split(c_ref[...])]
    want = jnp.concatenate([want[0] * 64.0 + want[1]] * 6, axis=0)

    _, _, part_tall = places((128, 20), 0)
    column = lax.broadcasted_iota(jnp.int32, (128, 20), 1)
    slots = []
    for x in split(near_ref[...]):
        for s in range(5):
            pick = (column == 5 * part_tall + s).astype(jnp.float32).astype(jnp.bfloat16)
            slots.append(exact(pick, x, ((1,), (0,))).astype(jnp.bfloat16))
    slots = jnp.concatenate(slots, axis=0)

    cols = jnp.zeros((48, 1280), jnp.float32)
    d = jnp.zeros((48, 128), jnp.int32)
    wide = jnp.concatenate([k_of] * 10, axis=1)
    for t in range(5):
        ids = jnp.concatenate([l_ref[:, 5 * g + t : 5 * g + t + 1] for g in range(6)], axis=0)
        hot = ids - start == lax.broadcasted_iota(jnp.int32, (48, near_ref.shape[1]), 1)
        hot = hot.astype(jnp.float32).astype(jnp.bfloat16)
        cols = jnp.where(wide == t, exact(hot, slots, ((1,), (1,))), cols)
        d = jnp.where(k_of == t, ids - first, d)

    remote = (part >> 1) != h
    inside = (d >= 0) & (d < 2 * HALF)
    piece = jnp.where(inside, (d >> 4) ^ h ^ 1, 2) * (2 * TILES)
    j = d & (HALF - 1)
    where = jnp.full((48, 128), ZERO, jnp.int32)
    for s in range(5):
        packed = 4 * j + s if s < 4 else 2 * TILES - HALF + j
        place = jnp.where(remote, piece + packed, jnp.where(inside, 6 * d + s, RAW + packed))
        got = cols[:, 128 * s : 128 * s + 128] * 64.0 + cols[:, 640 + 128 * s : 768 + 128 * s]
        where = jnp.where(got == want, place, where)
    tab_ref[...] = where ^ (m_of & 1)


def table(h, r, l_index, s_cols, c_index):
    total = s_cols.shape[0]
    first = 2 * HALF * r
    start = jnp.clip(first - HALF, 0, total - 4 * HALF)
    near = lax.dynamic_slice_in_dim(s_cols, start, 4 * HALF, axis=0).T
    vmem = pl.BlockSpec(memory_space=pltpu.VMEM)
    out = pl.pallas_call(
        table_body,
        out_shape=jax.ShapeDtypeStruct((48, 128), jnp.int32),
        in_specs=[pl.BlockSpec(memory_space=pltpu.SMEM), vmem, vmem, vmem],
        out_specs=vmem,
        compiler_params=pltpu.CompilerParams(vmem_limit_bytes=8 << 20),
        cost_estimate=pl.CostEstimate(flops=1 << 28, bytes_accessed=8 << 20, transcendentals=0),
    )(jnp.stack([start, first, h]), near, l_index, c_index)
    return out.reshape(48 * 128)


def shards(l_blocks, s_blocks, l_index, s_cols, c_index):
    r, c = lax.axis_index("rows"), lax.axis_index("cols")
    groups = lax.axis_size("rows")
    h = c // 2
    across = functools.partial(lax.ppermute, axis_name="cols", perm=[(k, k ^ 2) for k in range(4)])
    beside = functools.partial(lax.ppermute, axis_name="cols", perm=[(k, k ^ 1) for k in range(4)])
    up = [(4 * g + k, 4 * g + 4 + k) for g in range(groups - 1) for k in (0, 1)]
    down = [(4 * g + k, 4 * g - 4 + k) for g in range(1, groups) for k in (2, 3)]
    below, above = groups // 2 - 1, groups // 2
    seam = [(4 * below + 2 + k, 4 * above + k) for k in (0, 1)]
    seam += [(4 * above + k, 4 * below + 2 + k) for k in (0, 1)]
    plain = [route for route in up + down if route[1] not in {q for _, q in seam}]
    takes = ((r == above) & (h == 0)) | ((r == below) & (h == 1))

    def send(x, perm):
        return lax.ppermute(x, ("rows", "cols"), perm)

    first, second = pack(h.reshape(1), s_blocks)
    far_first = across(first)
    halo = send(second, up + down)
    seam_halo = send(first, seam)
    mate, first = lax.optimization_barrier((s_blocks, first))
    mate = beside(mate)
    tab = table(h, r, l_index, s_cols, c_index)
    second, halo, tab = lax.optimization_barrier((second, halo, tab))
    far_second = across(second)

    far_halo = send(far_first, plain)
    cross_first = beside(far_first)
    mate_halo = beside(halo)
    tab, far_first, seam_halo = lax.optimization_barrier((tab, far_first, seam_halo))
    parts = [(c ^ flip).reshape(1) for flip in range(4)]
    out = product(tab, parts[0], l_blocks, (s_blocks, halo), None)
    out = product(tab, parts[1], l_blocks, (mate, mate_halo), out)
    out, far_second, far_halo = lax.optimization_barrier((out, far_second, far_halo))
    cross_second = beside(far_second)
    far_halo = jnp.where(takes, seam_halo, far_halo)
    cross_halo = beside(far_halo)
    out = product(tab, parts[2], l_blocks, (far_first, far_second, far_halo), out)
    return product(tab, parts[3], l_blocks, (cross_first, cross_second, cross_halo), out)


def solution(mesh):
    return jax.shard_map(
        shards,
        mesh=mesh,
        in_specs=(
            P(("rows", "cols"), None, None),
            P("rows", None, "cols"),
            P(("rows", "cols"), None),
            P(),
            P(("rows", "cols"), None),
        ),
        out_specs=P(("rows", "cols"), None, None),
        check_vma=False,
    )
```

```python
import functools

import jax
import jax.numpy as jnp
from jax import lax
from jax.experimental import pallas as pl
from jax.experimental.pallas import tpu as pltpu
from jax.sharding import PartitionSpec as P

HALF = 16
TILES = 40
RAW = 6 * 2 * HALF
ZERO = RAW + 2 * TILES


def pack_body(start_ref, s_ref, first_ref, second_ref):
    def row(j, carry):
        for out_ref, base in places:
            for t in range(2):
                out_ref[2 * j + t] = s_ref[base + j, :, 128 * t : 128 * t + 128]
        return carry

    def pair(j, carry):
        for out_ref, base in places:
            out_ref[32 + j] = jnp.concatenate(
                [s_ref[base + 2 * j, :, 256:320], s_ref[base + 2 * j + 1, :, 256:320]], axis=1
            )
        return carry

    places = ((first_ref, HALF * start_ref[0]), (second_ref, HALF * (1 - start_ref[0])))
    lax.fori_loop(0, HALF, row, 0, unroll=4)
    lax.fori_loop(0, HALF // 2, pair, 0, unroll=4)


def pack(start, s_blocks):
    piece = jax.ShapeDtypeStruct((TILES, 64, 128), jnp.bfloat16)
    vmem = pl.BlockSpec(memory_space=pltpu.VMEM)
    return pl.pallas_call(
        pack_body,
        out_shape=(piece, piece),
        in_specs=[pl.BlockSpec(memory_space=pltpu.SMEM), vmem],
        out_specs=(vmem,) * 2,
        compiler_params=pltpu.CompilerParams(vmem_limit_bytes=16 << 20),
        cost_estimate=pl.CostEstimate(flops=0, bytes_accessed=3 << 20, transcendentals=0),
    )(start, s_blocks)


def product_body(count, tab_ref, part_ref, l_ref, *rest):
    o_ref, sd_ref, ob_ref, sem = rest[-4:]
    rows = l_ref.shape[0]
    base = 0
    for piece in rest[:count]:
        packed = piece.shape[2] == 128

        def spread(t, carry, piece=piece, base=base, packed=packed):
            for u in range(1 if packed else 2):
                v = piece[t, :, 128 * u : 128 * u + 128]
                at = base + 2 * t if packed else base + 6 * t + 2 * u
                sd_ref[at] = v
                sd_ref[at + 1] = jnp.concatenate([v[:, 64:], v[:, :64]], axis=1)
            if not packed:
                v = piece[t, :, 256:320]
                v = jnp.concatenate([v, v], axis=1)
                sd_ref[base + 6 * t + 4] = v
                sd_ref[base + 6 * t + 5] = v
            return carry

        lax.fori_loop(0, piece.shape[0], spread, 0, unroll=8 if packed else 4)
        base += 2 * TILES if packed else RAW
    for zero in (ZERO, ZERO + 1):
        sd_ref[zero] = jnp.zeros((64, 128), jnp.bfloat16)
    part = part_ref[0]
    low = lax.broadcasted_iota(jnp.int32, (64, 128), 1) < 64

    def out(i):
        lanes = pl.ds(pl.multiple_of(part * 384, 128), 384)
        return pltpu.make_async_copy(ob_ref.at[i], o_ref.at[i, :, lanes], sem.at[i])

    def row(i, carry):
        def pick(k, m):
            at = (k // 5 * 8 + i) * 128 + k % 5 * 24 + part * 6 + 2 * m
            return jnp.where(low, sd_ref[tab_ref[at]], sd_ref[tab_ref[at + 1]])

        total = jnp.zeros((64, 384), jnp.float32)
        for k0 in range(0, 30, 4):
            ks = range(k0, min(k0 + 4, 30))
            picked = jnp.concatenate(
                [jnp.concatenate([pick(k, m) for m in range(3)], axis=1) for k in ks], axis=0
            )
            total = total + jnp.dot(
                l_ref[i, :, 64 * k0 : 64 * (k0 + len(ks))], picked, preferred_element_type=jnp.float32
            )
        ob_ref[i] = total.astype(o_ref.dtype)
        out(i).start()
        return carry

    lax.fori_loop(0, rows, row, 0, unroll=True)

    def finish(i, carry):
        out(i).wait()
        return carry

    lax.fori_loop(0, rows, finish, 0)


def product(tab, part, l_blocks, pieces, prev):
    rows = l_blocks.shape[0]
    vmem, smem = pl.BlockSpec(memory_space=pltpu.VMEM), pl.BlockSpec(memory_space=pltpu.SMEM)
    in_specs = [smem, smem] + [vmem] * (1 + len(pieces))
    args = [tab, part, l_blocks, *pieces]
    aliases = {}
    if prev is not None:
        in_specs.append(pl.BlockSpec(memory_space=pl.ANY))
        aliases = {len(args): 0}
        args.append(prev)
    return pl.pallas_call(
        functools.partial(product_body, len(pieces)),
        out_shape=jax.ShapeDtypeStruct((rows, 64, 1536), jnp.bfloat16),
        in_specs=in_specs,
        out_specs=pl.BlockSpec(memory_space=pl.ANY),
        scratch_shapes=[
            pltpu.VMEM((ZERO + 2, 64, 128), jnp.bfloat16),
            pltpu.VMEM((rows, 64, 384), jnp.bfloat16),
            pltpu.SemaphoreType.DMA((rows,)),
        ],
        input_output_aliases=aliases,
        compiler_params=pltpu.CompilerParams(vmem_limit_bytes=24 << 20),
        cost_estimate=pl.CostEstimate(flops=755_000_000, bytes_accessed=20 << 20, transcendentals=0),
    )(*args)


def split(v):
    return [x.astype(jnp.float32).astype(jnp.bfloat16) for x in (v >> 6, v & 63)]


def exact(a, b, dims):
    return lax.dot_general(a, b, (dims, ((), ())), preferred_element_type=jnp.float32)


def table_body(at_ref, near_ref, l_ref, c_ref, tab_ref):
    start, first, h = at_ref[0], at_ref[1], at_ref[2]

    def places(shape, dim):
        lane = lax.broadcasted_iota(jnp.int32, shape, dim)
        k = sum((lane >= 24 * t).astype(jnp.int32) for t in range(1, 5))
        m = lane - 24 * k
        return k, m, sum((m >= 6 * t).astype(jnp.int32) for t in range(1, 4))

    k_of, m_of, part = places((48, 128), 1)
    _, m_wide, _ = places((24, 128), 1)
    tile = (lax.broadcasted_iota(jnp.int32, (24, 128), 0) == m_wide).astype(jnp.float32).astype(jnp.bfloat16)
    want = [exact(x, tile, ((1,), (0,))) for x in split(c_ref[...])]
    want = jnp.concatenate([want[0] * 64.0 + want[1]] * 6, axis=0)

    _, _, part_tall = places((128, 20), 0)
    column = lax.broadcasted_iota(jnp.int32, (128, 20), 1)
    slots = []
    for x in split(near_ref[...]):
        for s in range(5):
            pick = (column == 5 * part_tall + s).astype(jnp.float32).astype(jnp.bfloat16)
            slots.append(exact(pick, x, ((1,), (0,))).astype(jnp.bfloat16))
    slots = jnp.concatenate(slots, axis=0)

    cols = jnp.zeros((48, 1280), jnp.float32)
    d = jnp.zeros((48, 128), jnp.int32)
    wide = jnp.concatenate([k_of] * 10, axis=1)
    for t in range(5):
        ids = jnp.concatenate([l_ref[:, 5 * g + t : 5 * g + t + 1] for g in range(6)], axis=0)
        hot = ids - start == lax.broadcasted_iota(jnp.int32, (48, near_ref.shape[1]), 1)
        hot = hot.astype(jnp.float32).astype(jnp.bfloat16)
        cols = jnp.where(wide == t, exact(hot, slots, ((1,), (1,))), cols)
        d = jnp.where(k_of == t, ids - first, d)

    remote = (part >> 1) != h
    inside = (d >= 0) & (d < 2 * HALF)
    piece = jnp.where(inside, (d >> 4) ^ h ^ 1, 2) * (2 * TILES)
    j = d & (HALF - 1)
    where = jnp.full((48, 128), ZERO, jnp.int32)
    for s in range(5):
        packed = 4 * j + s if s < 4 else 2 * TILES - HALF + j
        place = jnp.where(remote, piece + packed, jnp.where(inside, 6 * d + s, RAW + packed))
        got = cols[:, 128 * s : 128 * s + 128] * 64.0 + cols[:, 640 + 128 * s : 768 + 128 * s]
        where = jnp.where(got == want, place, where)
    tab_ref[...] = where ^ (m_of & 1)


def table(h, r, l_index, s_cols, c_index):
    total = s_cols.shape[0]
    first = 2 * HALF * r
    start = jnp.clip(first - HALF, 0, total - 4 * HALF)
    near = lax.dynamic_slice_in_dim(s_cols, start, 4 * HALF, axis=0).T
    vmem = pl.BlockSpec(memory_space=pltpu.VMEM)
    out = pl.pallas_call(
        table_body,
        out_shape=jax.ShapeDtypeStruct((48, 128), jnp.int32),
        in_specs=[pl.BlockSpec(memory_space=pltpu.SMEM), vmem, vmem, vmem],
        out_specs=vmem,
        compiler_params=pltpu.CompilerParams(vmem_limit_bytes=8 << 20),
        cost_estimate=pl.CostEstimate(flops=1 << 28, bytes_accessed=8 << 20, transcendentals=0),
    )(jnp.stack([start, first, h]), near, l_index, c_index)
    return out.reshape(48 * 128)


def shards(l_blocks, s_blocks, l_index, s_cols, c_index):
    r, c = lax.axis_index("rows"), lax.axis_index("cols")
    groups = lax.axis_size("rows")
    h = c // 2
    across = functools.partial(lax.ppermute, axis_name="cols", perm=[(k, k ^ 2) for k in range(4)])
    beside = functools.partial(lax.ppermute, axis_name="cols", perm=[(k, k ^ 1) for k in range(4)])
    up = [(4 * g + k, 4 * g + 4 + k) for g in range(groups - 1) for k in (0, 1)]
    down = [(4 * g + k, 4 * g - 4 + k) for g in range(1, groups) for k in (2, 3)]
    below, above = groups // 2 - 1, groups // 2
    seam = [(4 * below + 2 + k, 4 * above + k) for k in (0, 1)]
    seam += [(4 * above + k, 4 * below + 2 + k) for k in (0, 1)]
    plain = [route for route in up + down if route[1] not in {q for _, q in seam}]
    takes = ((r == above) & (h == 0)) | ((r == below) & (h == 1))

    def send(x, perm):
        return lax.ppermute(x, ("rows", "cols"), perm)

    first, second = pack(h.reshape(1), s_blocks)
    far_first = across(first)
    halo = send(second, up + down)
    seam_halo = send(first, seam)
    mate, first = lax.optimization_barrier((s_blocks, first))
    mate = beside(mate)
    tab = table(h, r, l_index, s_cols, c_index)
    second, far_first, tab = lax.optimization_barrier((second, far_first, tab))
    far_second = across(second)
    far_halo = send(far_first, plain)
    cross_first = beside(far_first)
    halo, far_first = lax.optimization_barrier((halo, far_first))
    mate_halo = beside(halo)
    parts = [(c ^ flip).reshape(1) for flip in range(4)]
    out = product(tab, parts[0], l_blocks, (s_blocks, halo), None)
    out, mate, seam_halo = lax.optimization_barrier((out, mate, seam_halo))
    out = product(tab, parts[1], l_blocks, (mate, mate_halo), out)
    out, far_second, far_halo = lax.optimization_barrier((out, far_second, far_halo))
    cross_second = beside(far_second)
    far_halo = jnp.where(takes, seam_halo, far_halo)
    cross_halo = beside(far_halo)
    out = product(tab, parts[2], l_blocks, (far_first, far_second, far_halo), out)
    return product(tab, parts[3], l_blocks, (cross_first, cross_second, cross_halo), out)


def solution(mesh):
    return jax.shard_map(
        shards,
        mesh=mesh,
        in_specs=(
            P(("rows", "cols"), None, None),
            P("rows", None, "cols"),
            P(("rows", "cols"), None),
            P(),
            P(("rows", "cols"), None),
        ),
        out_specs=P(("rows", "cols"), None, None),
        check_vma=False,
    )
```

```python
import functools

import jax
import jax.numpy as jnp
from jax import lax
from jax.experimental import pallas as pl
from jax.experimental.pallas import tpu as pltpu
from jax.sharding import PartitionSpec as P

HALF = 16
TILES = 40
RAW = 6 * 2 * HALF
ZERO = RAW + 2 * TILES


def pack_body(start_ref, s_ref, first_ref, second_ref):
    def row(j, carry):
        for out_ref, base in places:
            for t in range(2):
                out_ref[2 * j + t] = s_ref[base + j, :, 128 * t : 128 * t + 128]
        return carry

    def pair(j, carry):
        for out_ref, base in places:
            out_ref[32 + j] = jnp.concatenate(
                [s_ref[base + 2 * j, :, 256:320], s_ref[base + 2 * j + 1, :, 256:320]], axis=1
            )
        return carry

    places = ((first_ref, HALF * start_ref[0]), (second_ref, HALF * (1 - start_ref[0])))
    lax.fori_loop(0, HALF, row, 0, unroll=4)
    lax.fori_loop(0, HALF // 2, pair, 0, unroll=4)


def pack(start, s_blocks):
    piece = jax.ShapeDtypeStruct((TILES, 64, 128), jnp.bfloat16)
    vmem = pl.BlockSpec(memory_space=pltpu.VMEM)
    return pl.pallas_call(
        pack_body,
        out_shape=(piece, piece),
        in_specs=[pl.BlockSpec(memory_space=pltpu.SMEM), vmem],
        out_specs=(vmem,) * 2,
        compiler_params=pltpu.CompilerParams(vmem_limit_bytes=16 << 20),
        cost_estimate=pl.CostEstimate(flops=0, bytes_accessed=3 << 20, transcendentals=0),
    )(start, s_blocks)


def product_body(count, tab_ref, part_ref, l_ref, *rest):
    o_ref, sd_ref, ob_ref, sem = rest[-4:]
    rows = l_ref.shape[0]
    base = 0
    for piece in rest[:count]:
        packed = piece.shape[2] == 128

        def spread(t, carry, piece=piece, base=base, packed=packed):
            for u in range(1 if packed else 2):
                v = piece[t, :, 128 * u : 128 * u + 128]
                at = base + 2 * t if packed else base + 6 * t + 2 * u
                sd_ref[at] = v
                sd_ref[at + 1] = jnp.concatenate([v[:, 64:], v[:, :64]], axis=1)
            if not packed:
                v = piece[t, :, 256:320]
                v = jnp.concatenate([v, v], axis=1)
                sd_ref[base + 6 * t + 4] = v
                sd_ref[base + 6 * t + 5] = v
            return carry

        lax.fori_loop(0, piece.shape[0], spread, 0, unroll=8 if packed else 4)
        base += 2 * TILES if packed else RAW
    for zero in (ZERO, ZERO + 1):
        sd_ref[zero] = jnp.zeros((64, 128), jnp.bfloat16)
    part = part_ref[0]
    low = lax.broadcasted_iota(jnp.int32, (64, 128), 1) < 64

    def out(i):
        lanes = pl.ds(pl.multiple_of(part * 384, 128), 384)
        return pltpu.make_async_copy(ob_ref.at[i], o_ref.at[i, :, lanes], sem.at[i])

    def row(i, carry):
        def pick(k, m):
            at = (k // 5 * 8 + i) * 128 + k % 5 * 24 + part * 6 + 2 * m
            return jnp.where(low, sd_ref[tab_ref[at]], sd_ref[tab_ref[at + 1]])

        total = jnp.zeros((64, 384), jnp.float32)
        for k0 in range(0, 30, 4):
            ks = range(k0, min(k0 + 4, 30))
            picked = jnp.concatenate(
                [jnp.concatenate([pick(k, m) for m in range(3)], axis=1) for k in ks], axis=0
            )
            total = total + jnp.dot(
                l_ref[i, :, 64 * k0 : 64 * (k0 + len(ks))], picked, preferred_element_type=jnp.float32
            )
        ob_ref[i] = total.astype(o_ref.dtype)
        out(i).start()
        return carry

    lax.fori_loop(0, rows, row, 0, unroll=True)

    def finish(i, carry):
        out(i).wait()
        return carry

    lax.fori_loop(0, rows, finish, 0)


def product(tab, part, l_blocks, pieces, prev):
    rows = l_blocks.shape[0]
    vmem, smem = pl.BlockSpec(memory_space=pltpu.VMEM), pl.BlockSpec(memory_space=pltpu.SMEM)
    in_specs = [smem, smem] + [vmem] * (1 + len(pieces))
    args = [tab, part, l_blocks, *pieces]
    aliases = {}
    if prev is not None:
        in_specs.append(pl.BlockSpec(memory_space=pl.ANY))
        aliases = {len(args): 0}
        args.append(prev)
    return pl.pallas_call(
        functools.partial(product_body, len(pieces)),
        out_shape=jax.ShapeDtypeStruct((rows, 64, 1536), jnp.bfloat16),
        in_specs=in_specs,
        out_specs=pl.BlockSpec(memory_space=pl.ANY),
        scratch_shapes=[
            pltpu.VMEM((ZERO + 2, 64, 128), jnp.bfloat16),
            pltpu.VMEM((rows, 64, 384), jnp.bfloat16),
            pltpu.SemaphoreType.DMA((rows,)),
        ],
        input_output_aliases=aliases,
        compiler_params=pltpu.CompilerParams(vmem_limit_bytes=24 << 20),
        cost_estimate=pl.CostEstimate(flops=755_000_000, bytes_accessed=20 << 20, transcendentals=0),
    )(*args)


def split(v):
    return [x.astype(jnp.float32).astype(jnp.bfloat16) for x in (v >> 6, v & 63)]


def exact(a, b, dims):
    return lax.dot_general(a, b, (dims, ((), ())), preferred_element_type=jnp.float32)


def table_body(at_ref, near_ref, l_ref, c_ref, tab_ref):
    start, first, h = at_ref[0], at_ref[1], at_ref[2]

    def places(shape, dim):
        lane = lax.broadcasted_iota(jnp.int32, shape, dim)
        k = sum((lane >= 24 * t).astype(jnp.int32) for t in range(1, 5))
        m = lane - 24 * k
        return k, m, sum((m >= 6 * t).astype(jnp.int32) for t in range(1, 4))

    k_of, m_of, part = places((48, 128), 1)
    _, m_wide, _ = places((24, 128), 1)
    tile = (lax.broadcasted_iota(jnp.int32, (24, 128), 0) == m_wide).astype(jnp.float32).astype(jnp.bfloat16)
    want = [exact(x, tile, ((1,), (0,))) for x in split(c_ref[...])]
    want = jnp.concatenate([want[0] * 64.0 + want[1]] * 6, axis=0)

    _, _, part_tall = places((128, 20), 0)
    column = lax.broadcasted_iota(jnp.int32, (128, 20), 1)
    slots = []
    for x in split(near_ref[...]):
        for s in range(5):
            pick = (column == 5 * part_tall + s).astype(jnp.float32).astype(jnp.bfloat16)
            slots.append(exact(pick, x, ((1,), (0,))).astype(jnp.bfloat16))
    slots = jnp.concatenate(slots, axis=0)

    cols = jnp.zeros((48, 1280), jnp.float32)
    d = jnp.zeros((48, 128), jnp.int32)
    wide = jnp.concatenate([k_of] * 10, axis=1)
    for t in range(5):
        ids = jnp.concatenate([l_ref[:, 5 * g + t : 5 * g + t + 1] for g in range(6)], axis=0)
        hot = ids - start == lax.broadcasted_iota(jnp.int32, (48, near_ref.shape[1]), 1)
        hot = hot.astype(jnp.float32).astype(jnp.bfloat16)
        cols = jnp.where(wide == t, exact(hot, slots, ((1,), (1,))), cols)
        d = jnp.where(k_of == t, ids - first, d)

    remote = (part >> 1) != h
    inside = (d >= 0) & (d < 2 * HALF)
    piece = jnp.where(inside, (d >> 4) ^ h ^ 1, 2) * (2 * TILES)
    j = d & (HALF - 1)
    where = jnp.full((48, 128), ZERO, jnp.int32)
    for s in range(5):
        packed = 4 * j + s if s < 4 else 2 * TILES - HALF + j
        place = jnp.where(remote, piece + packed, jnp.where(inside, 6 * d + s, RAW + packed))
        got = cols[:, 128 * s : 128 * s + 128] * 64.0 + cols[:, 640 + 128 * s : 768 + 128 * s]
        where = jnp.where(got == want, place, where)
    tab_ref[...] = where ^ (m_of & 1)


def table(h, r, l_index, s_cols, c_index):
    total = s_cols.shape[0]
    first = 2 * HALF * r
    start = jnp.clip(first - HALF, 0, total - 4 * HALF)
    near = lax.dynamic_slice_in_dim(s_cols, start, 4 * HALF, axis=0).T
    vmem = pl.BlockSpec(memory_space=pltpu.VMEM)
    out = pl.pallas_call(
        table_body,
        out_shape=jax.ShapeDtypeStruct((48, 128), jnp.int32),
        in_specs=[pl.BlockSpec(memory_space=pltpu.SMEM), vmem, vmem, vmem],
        out_specs=vmem,
        compiler_params=pltpu.CompilerParams(vmem_limit_bytes=8 << 20),
        cost_estimate=pl.CostEstimate(flops=1 << 28, bytes_accessed=8 << 20, transcendentals=0),
    )(jnp.stack([start, first, h]), near, l_index, c_index)
    return out.reshape(48 * 128)


def shards(l_blocks, s_blocks, l_index, s_cols, c_index):
    r, c = lax.axis_index("rows"), lax.axis_index("cols")
    groups = lax.axis_size("rows")
    h = c // 2
    across = functools.partial(lax.ppermute, axis_name="cols", perm=[(k, k ^ 2) for k in range(4)])
    beside = functools.partial(lax.ppermute, axis_name="cols", perm=[(k, k ^ 1) for k in range(4)])
    up = [(4 * g + k, 4 * g + 4 + k) for g in range(groups - 1) for k in (0, 1)]
    down = [(4 * g + k, 4 * g - 4 + k) for g in range(1, groups) for k in (2, 3)]
    below, above, last = groups // 2 - 1, groups // 2, groups - 1
    seam = [(4 * below + 2 + k, 4 * above + k) for k in (0, 1)]
    seam += [(4 * above + k, 4 * below + 2 + k) for k in (0, 1)]
    plain = [route for route in up + down if route[1] not in {q for _, q in seam}]
    direct = [(4 * below + k, 4 * above + k) for k in (0, 1)]
    direct += [(4 * above + 2 + k, 4 * below + 2 + k) for k in (0, 1)]
    relay = [(4 * below + k, 4 * last + k) for k in (0, 1)] + [(4 * above + 2 + k, 2 + k) for k in (0, 1)]
    onward = [(4 * last + k, 4 * above + k) for k in (0, 1)] + [(2 + k, 4 * below + 2 + k) for k in (0, 1)]
    takes = ((r == above) & (h == 0)) | ((r == below) & (h == 1))

    def send(x, perm):
        return lax.ppermute(x, ("rows", "cols"), perm)

    first, second = pack(h.reshape(1), s_blocks)
    far_first = across(first)
    halo = send(second, plain)
    relayed = send(second[TILES // 2 :], relay)
    seam_first = send(second[: TILES // 2], direct)
    seam_halo = send(first, seam)
    mate, first = lax.optimization_barrier((s_blocks, first))
    mate = beside(mate)
    c_index, relayed = lax.optimization_barrier((c_index, relayed))
    seam_second = send(relayed, onward)
    tab = table(h, r, l_index, s_cols, c_index)
    second, far_first, tab = lax.optimization_barrier((second, far_first, tab))
    far_second = across(second)
    far_halo = send(far_first, plain)
    cross_first = beside(far_first)
    halo, far_first = lax.optimization_barrier((halo, far_first))
    halo = jnp.where(takes, jnp.concatenate([seam_first, seam_second]), halo)
    mate_halo = beside(halo)
    parts = [(c ^ flip).reshape(1) for flip in range(4)]
    out = product(tab, parts[0], l_blocks, (s_blocks, halo), None)
    out, mate, seam_halo = lax.optimization_barrier((out, mate, seam_halo))
    out = product(tab, parts[1], l_blocks, (mate, mate_halo), out)
    out, far_second, far_halo = lax.optimization_barrier((out, far_second, far_halo))
    cross_second = beside(far_second)
    far_halo = jnp.where(takes, seam_halo, far_halo)
    cross_halo = beside(far_halo)
    out = product(tab, parts[2], l_blocks, (far_first, far_second, far_halo), out)
    return product(tab, parts[3], l_blocks, (cross_first, cross_second, cross_halo), out)


def solution(mesh):
    return jax.shard_map(
        shards,
        mesh=mesh,
        in_specs=(
            P(("rows", "cols"), None, None),
            P("rows", None, "cols"),
            P(("rows", "cols"), None),
            P(),
            P(("rows", "cols"), None),
        ),
        out_specs=P(("rows", "cols"), None, None),
        check_vma=False,
    )
```

```python
import functools

import jax
import jax.numpy as jnp
from jax import lax
from jax.experimental import pallas as pl
from jax.experimental.pallas import tpu as pltpu
from jax.sharding import PartitionSpec as P

HALF = 16
TILES = 40
RAW = 6 * 2 * HALF
ZERO = RAW + 2 * TILES


def pack_body(start_ref, s_ref, first_ref, second_ref):
    def row(j, carry):
        for out_ref, base in places:
            for t in range(2):
                out_ref[2 * j + t] = s_ref[base + j, :, 128 * t : 128 * t + 128]
        return carry

    def pair(j, carry):
        for out_ref, base in places:
            out_ref[32 + j] = jnp.concatenate(
                [s_ref[base + 2 * j, :, 256:320], s_ref[base + 2 * j + 1, :, 256:320]], axis=1
            )
        return carry

    places = ((first_ref, HALF * start_ref[0]), (second_ref, HALF * (1 - start_ref[0])))
    lax.fori_loop(0, HALF, row, 0, unroll=4)
    lax.fori_loop(0, HALF // 2, pair, 0, unroll=4)


def pack(start, s_blocks):
    piece = jax.ShapeDtypeStruct((TILES, 64, 128), jnp.bfloat16)
    vmem = pl.BlockSpec(memory_space=pltpu.VMEM)
    return pl.pallas_call(
        pack_body,
        out_shape=(piece, piece),
        in_specs=[pl.BlockSpec(memory_space=pltpu.SMEM), vmem],
        out_specs=(vmem,) * 2,
        compiler_params=pltpu.CompilerParams(vmem_limit_bytes=16 << 20),
        cost_estimate=pl.CostEstimate(flops=0, bytes_accessed=3 << 20, transcendentals=0),
    )(start, s_blocks)


def product_body(count, tab_hbm, part_ref, l_ref, *rest):
    o_ref, sd_ref, ob_ref, tab_ref, sem, tab_sem = rest[-6:]
    load = pltpu.make_async_copy(tab_hbm, tab_ref, tab_sem)
    load.start()
    rows = l_ref.shape[0]
    base = 0
    for piece in rest[:count]:
        packed = piece.shape[2] == 128

        def spread(t, carry, piece=piece, base=base, packed=packed):
            for u in range(1 if packed else 2):
                v = piece[t, :, 128 * u : 128 * u + 128]
                at = base + 2 * t if packed else base + 6 * t + 2 * u
                sd_ref[at] = v
                sd_ref[at + 1] = jnp.concatenate([v[:, 64:], v[:, :64]], axis=1)
            if not packed:
                v = piece[t, :, 256:320]
                v = jnp.concatenate([v, v], axis=1)
                sd_ref[base + 6 * t + 4] = v
                sd_ref[base + 6 * t + 5] = v
            return carry

        lax.fori_loop(0, piece.shape[0], spread, 0, unroll=8 if packed else 4)
        base += 2 * TILES if packed else RAW
    for zero in (ZERO, ZERO + 1):
        sd_ref[zero] = jnp.zeros((64, 128), jnp.bfloat16)
    load.wait()
    part = part_ref[0]
    low = lax.broadcasted_iota(jnp.int32, (64, 128), 1) < 64

    def out(i):
        lanes = pl.ds(pl.multiple_of(part * 384, 128), 384)
        return pltpu.make_async_copy(ob_ref.at[i], o_ref.at[i, :, lanes], sem.at[i])

    def row(i, carry):
        def pick(k, m):
            at = (k // 5 * 8 + i) * 128 + k % 5 * 24 + part * 6 + 2 * m
            return jnp.where(low, sd_ref[tab_ref[at]], sd_ref[tab_ref[at + 1]])

        total = jnp.zeros((64, 384), jnp.float32)
        for k0 in range(0, 30, 4):
            ks = range(k0, min(k0 + 4, 30))
            picked = jnp.concatenate(
                [jnp.concatenate([pick(k, m) for m in range(3)], axis=1) for k in ks], axis=0
            )
            total = total + jnp.dot(
                l_ref[i, :, 64 * k0 : 64 * (k0 + len(ks))], picked, preferred_element_type=jnp.float32
            )
        ob_ref[i] = total.astype(o_ref.dtype)
        out(i).start()
        return carry

    lax.fori_loop(0, rows, row, 0, unroll=True)

    def finish(i, carry):
        out(i).wait()
        return carry

    lax.fori_loop(0, rows, finish, 0)


def product(tab, part, l_blocks, pieces, prev):
    rows = l_blocks.shape[0]
    vmem, smem = pl.BlockSpec(memory_space=pltpu.VMEM), pl.BlockSpec(memory_space=pltpu.SMEM)
    in_specs = [pl.BlockSpec(memory_space=pl.ANY), smem] + [vmem] * (1 + len(pieces))
    args = [tab, part, l_blocks, *pieces]
    aliases = {}
    if prev is not None:
        in_specs.append(pl.BlockSpec(memory_space=pl.ANY))
        aliases = {len(args): 0}
        args.append(prev)
    return pl.pallas_call(
        functools.partial(product_body, len(pieces)),
        out_shape=jax.ShapeDtypeStruct((rows, 64, 1536), jnp.bfloat16),
        in_specs=in_specs,
        out_specs=pl.BlockSpec(memory_space=pl.ANY),
        scratch_shapes=[
            pltpu.VMEM((ZERO + 2, 64, 128), jnp.bfloat16),
            pltpu.VMEM((rows, 64, 384), jnp.bfloat16),
            pltpu.SMEM(tab.shape, jnp.int32),
            pltpu.SemaphoreType.DMA((rows,)),
            pltpu.SemaphoreType.DMA,
        ],
        input_output_aliases=aliases,
        compiler_params=pltpu.CompilerParams(vmem_limit_bytes=24 << 20),
        cost_estimate=pl.CostEstimate(flops=755_000_000, bytes_accessed=20 << 20, transcendentals=0),
    )(*args)


def split(v):
    return [x.astype(jnp.float32).astype(jnp.bfloat16) for x in (v >> 6, v & 63)]


def exact(a, b, dims):
    return lax.dot_general(a, b, (dims, ((), ())), preferred_element_type=jnp.float32)


def table_body(at_ref, near_ref, l_ref, c_ref, tab_ref):
    start, first, h = at_ref[0], at_ref[1], at_ref[2]

    def places(shape, dim):
        lane = lax.broadcasted_iota(jnp.int32, shape, dim)
        k = sum((lane >= 24 * t).astype(jnp.int32) for t in range(1, 5))
        m = lane - 24 * k
        return k, m, sum((m >= 6 * t).astype(jnp.int32) for t in range(1, 4))

    k_of, m_of, part = places((48, 128), 1)
    _, m_wide, _ = places((24, 128), 1)
    tile = (lax.broadcasted_iota(jnp.int32, (24, 128), 0) == m_wide).astype(jnp.float32).astype(jnp.bfloat16)
    want = [exact(x, tile, ((1,), (0,))) for x in split(c_ref[...])]
    want = jnp.concatenate([want[0] * 64.0 + want[1]] * 6, axis=0)

    _, _, part_tall = places((128, 20), 0)
    column = lax.broadcasted_iota(jnp.int32, (128, 20), 1)
    slots = []
    for x in split(near_ref[...]):
        for s in range(5):
            pick = (column == 5 * part_tall + s).astype(jnp.float32).astype(jnp.bfloat16)
            slots.append(exact(pick, x, ((1,), (0,))).astype(jnp.bfloat16))
    slots = jnp.concatenate(slots, axis=0)

    cols = jnp.zeros((48, 1280), jnp.float32)
    d = jnp.zeros((48, 128), jnp.int32)
    wide = jnp.concatenate([k_of] * 10, axis=1)
    for t in range(5):
        ids = jnp.concatenate([l_ref[:, 5 * g + t : 5 * g + t + 1] for g in range(6)], axis=0)
        hot = ids - start == lax.broadcasted_iota(jnp.int32, (48, near_ref.shape[1]), 1)
        hot = hot.astype(jnp.float32).astype(jnp.bfloat16)
        cols = jnp.where(wide == t, exact(hot, slots, ((1,), (1,))), cols)
        d = jnp.where(k_of == t, ids - first, d)

    remote = (part >> 1) != h
    inside = (d >= 0) & (d < 2 * HALF)
    piece = jnp.where(inside, (d >> 4) ^ h ^ 1, 2) * (2 * TILES)
    j = d & (HALF - 1)
    where = jnp.full((48, 128), ZERO, jnp.int32)
    for s in range(5):
        packed = 4 * j + s if s < 4 else 2 * TILES - HALF + j
        place = jnp.where(remote, piece + packed, jnp.where(inside, 6 * d + s, RAW + packed))
        got = cols[:, 128 * s : 128 * s + 128] * 64.0 + cols[:, 640 + 128 * s : 768 + 128 * s]
        where = jnp.where(got == want, place, where)
    tab_ref[...] = where ^ (m_of & 1)


def table(h, r, l_index, s_cols, c_index):
    total = s_cols.shape[0]
    first = 2 * HALF * r
    start = jnp.clip(first - HALF, 0, total - 4 * HALF)
    near = lax.dynamic_slice_in_dim(s_cols, start, 4 * HALF, axis=0).T
    vmem = pl.BlockSpec(memory_space=pltpu.VMEM)
    out = pl.pallas_call(
        table_body,
        out_shape=jax.ShapeDtypeStruct((48, 128), jnp.int32),
        in_specs=[pl.BlockSpec(memory_space=pltpu.SMEM), vmem, vmem, vmem],
        out_specs=vmem,
        compiler_params=pltpu.CompilerParams(vmem_limit_bytes=8 << 20),
        cost_estimate=pl.CostEstimate(flops=1 << 28, bytes_accessed=8 << 20, transcendentals=0),
    )(jnp.stack([start, first, h]), near, l_index, c_index)
    return out.reshape(48 * 128)


def shards(l_blocks, s_blocks, l_index, s_cols, c_index):
    r, c = lax.axis_index("rows"), lax.axis_index("cols")
    groups = lax.axis_size("rows")
    h = c // 2
    across = functools.partial(lax.ppermute, axis_name="cols", perm=[(k, k ^ 2) for k in range(4)])
    beside = functools.partial(lax.ppermute, axis_name="cols", perm=[(k, k ^ 1) for k in range(4)])
    up = [(4 * g + k, 4 * g + 4 + k) for g in range(groups - 1) for k in (0, 1)]
    down = [(4 * g + k, 4 * g - 4 + k) for g in range(1, groups) for k in (2, 3)]
    below, above = groups // 2 - 1, groups // 2
    seam = [(4 * below + 2 + k, 4 * above + k) for k in (0, 1)]
    seam += [(4 * above + k, 4 * below + 2 + k) for k in (0, 1)]
    plain = [route for route in up + down if route[1] not in {q for _, q in seam}]
    takes = ((r == above) & (h == 0)) | ((r == below) & (h == 1))

    def send(x, perm):
        return lax.ppermute(x, ("rows", "cols"), perm)

    first, second = pack(h.reshape(1), s_blocks)
    far_first = across(first)
    halo = send(second, up + down)
    seam_halo = send(first, seam)
    mate, first = lax.optimization_barrier((s_blocks, first))
    mate = beside(mate)
    tab = table(h, r, l_index, s_cols, c_index)
    second, halo, tab = lax.optimization_barrier((second, halo, tab))
    far_second = across(second)
    mate_halo = beside(halo)
    parts = [(c ^ flip).reshape(1) for flip in range(4)]
    out = product(tab, parts[0], l_blocks, (s_blocks, halo), None)
    out, far_first = lax.optimization_barrier((out, far_first))
    far_halo = send(far_first, plain)
    cross_first = beside(far_first)
    out = product(tab, parts[1], l_blocks, (mate, mate_halo), out)
    out, far_second, far_halo, seam_halo = lax.optimization_barrier((out, far_second, far_halo, seam_halo))
    cross_second = beside(far_second)
    far_halo = jnp.where(takes, seam_halo, far_halo)
    cross_halo = beside(far_halo)
    out = product(tab, parts[2], l_blocks, (far_first, far_second, far_halo), out)
    return product(tab, parts[3], l_blocks, (cross_first, cross_second, cross_halo), out)


def solution(mesh):
    return jax.shard_map(
        shards,
        mesh=mesh,
        in_specs=(
            P(("rows", "cols"), None, None),
            P("rows", None, "cols"),
            P(("rows", "cols"), None),
            P(),
            P(("rows", "cols"), None),
        ),
        out_specs=P(("rows", "cols"), None, None),
        check_vma=False,
    )
```

```python
import functools

import jax
import jax.numpy as jnp
from jax import lax
from jax.experimental import pallas as pl
from jax.experimental.pallas import tpu as pltpu
from jax.sharding import PartitionSpec as P

HALF = 16
TILES = 40
RAW = 6 * 2 * HALF
ZERO = RAW + 2 * TILES


def pack_body(start_ref, s_ref, first_ref, second_ref):
    def row(j, carry):
        for out_ref, base in places:
            for t in range(2):
                out_ref[2 * j + t] = s_ref[base + j, :, 128 * t : 128 * t + 128]
        return carry

    def pair(j, carry):
        for out_ref, base in places:
            out_ref[32 + j] = jnp.concatenate(
                [s_ref[base + 2 * j, :, 256:320], s_ref[base + 2 * j + 1, :, 256:320]], axis=1
            )
        return carry

    places = ((first_ref, HALF * start_ref[0]), (second_ref, HALF * (1 - start_ref[0])))
    lax.fori_loop(0, HALF, row, 0, unroll=4)
    lax.fori_loop(0, HALF // 2, pair, 0, unroll=4)


def pack(start, s_blocks):
    piece = jax.ShapeDtypeStruct((TILES, 64, 128), jnp.bfloat16)
    vmem = pl.BlockSpec(memory_space=pltpu.VMEM)
    return pl.pallas_call(
        pack_body,
        out_shape=(piece, piece),
        in_specs=[pl.BlockSpec(memory_space=pltpu.SMEM), vmem],
        out_specs=(vmem,) * 2,
        compiler_params=pltpu.CompilerParams(vmem_limit_bytes=16 << 20),
        cost_estimate=pl.CostEstimate(flops=0, bytes_accessed=3 << 20, transcendentals=0),
    )(start, s_blocks)


def product_body(count, tab_ref, part_ref, l_ref, *rest):
    o_ref, sd_ref, ob_ref, sem = rest[-4:]
    rows = l_ref.shape[0]
    base = 0
    for piece in rest[:count]:
        packed = piece.shape[2] == 128

        def spread(t, carry, piece=piece, base=base, packed=packed):
            for u in range(1 if packed else 2):
                v = piece[t, :, 128 * u : 128 * u + 128]
                at = base + 2 * t if packed else base + 6 * t + 2 * u
                sd_ref[at] = v
                sd_ref[at + 1] = jnp.concatenate([v[:, 64:], v[:, :64]], axis=1)
            if not packed:
                v = piece[t, :, 256:320]
                v = jnp.concatenate([v, v], axis=1)
                sd_ref[base + 6 * t + 4] = v
                sd_ref[base + 6 * t + 5] = v
            return carry

        lax.fori_loop(0, piece.shape[0], spread, 0, unroll=8 if packed else 4)
        base += 2 * TILES if packed else RAW
    for zero in (ZERO, ZERO + 1):
        sd_ref[zero] = jnp.zeros((64, 128), jnp.bfloat16)
    part = part_ref[0]
    low = lax.broadcasted_iota(jnp.int32, (64, 128), 1) < 64

    def out(i):
        lanes = pl.ds(pl.multiple_of(part * 384, 128), 384)
        return pltpu.make_async_copy(ob_ref.at[i], o_ref.at[i, :, lanes], sem.at[i])

    def row(i, carry):
        def pick(k, m):
            at = (k // 5 * 8 + i) * 128 + k % 5 * 24 + part * 6 + 2 * m
            return jnp.where(low, sd_ref[tab_ref[at]], sd_ref[tab_ref[at + 1]])

        total = jnp.zeros((64, 384), jnp.float32)
        for k0 in range(0, 30, 4):
            ks = range(k0, min(k0 + 4, 30))
            picked = jnp.concatenate(
                [jnp.concatenate([pick(k, m) for m in range(3)], axis=1) for k in ks], axis=0
            )
            total = total + jnp.dot(
                l_ref[i, :, 64 * k0 : 64 * (k0 + len(ks))], picked, preferred_element_type=jnp.float32
            )
        ob_ref[i] = total.astype(o_ref.dtype)
        out(i).start()
        return carry

    lax.fori_loop(0, rows, row, 0, unroll=True)

    def finish(i, carry):
        out(i).wait()
        return carry

    lax.fori_loop(0, rows, finish, 0)


def product(tab, part, l_blocks, pieces, prev):
    rows = l_blocks.shape[0]
    vmem, smem = pl.BlockSpec(memory_space=pltpu.VMEM), pl.BlockSpec(memory_space=pltpu.SMEM)
    in_specs = [smem, smem] + [vmem] * (1 + len(pieces))
    args = [tab, part, l_blocks, *pieces]
    aliases = {}
    if prev is not None:
        in_specs.append(pl.BlockSpec(memory_space=pl.ANY))
        aliases = {len(args): 0}
        args.append(prev)
    return pl.pallas_call(
        functools.partial(product_body, len(pieces)),
        out_shape=jax.ShapeDtypeStruct((rows, 64, 1536), jnp.bfloat16),
        in_specs=in_specs,
        out_specs=pl.BlockSpec(memory_space=pl.ANY),
        scratch_shapes=[
            pltpu.VMEM((ZERO + 2, 64, 128), jnp.bfloat16),
            pltpu.VMEM((rows, 64, 384), jnp.bfloat16),
            pltpu.SemaphoreType.DMA((rows,)),
        ],
        input_output_aliases=aliases,
        compiler_params=pltpu.CompilerParams(vmem_limit_bytes=24 << 20),
        cost_estimate=pl.CostEstimate(flops=755_000_000, bytes_accessed=20 << 20, transcendentals=0),
    )(*args)


def split(v):
    return [x.astype(jnp.float32).astype(jnp.bfloat16) for x in (v >> 6, v & 63)]


def exact(a, b, dims):
    return lax.dot_general(a, b, (dims, ((), ())), preferred_element_type=jnp.float32)


def table_body(at_ref, near_ref, l_ref, c_ref, tab_ref):
    start, first, h = at_ref[0], at_ref[1], at_ref[2]

    def places(shape, dim):
        lane = lax.broadcasted_iota(jnp.int32, shape, dim)
        k = sum((lane >= 24 * t).astype(jnp.int32) for t in range(1, 5))
        m = lane - 24 * k
        return k, m, sum((m >= 6 * t).astype(jnp.int32) for t in range(1, 4))

    k_of, m_of, part = places((48, 128), 1)
    _, m_wide, _ = places((24, 128), 1)
    tile = (lax.broadcasted_iota(jnp.int32, (24, 128), 0) == m_wide).astype(jnp.float32).astype(jnp.bfloat16)
    want = [exact(x, tile, ((1,), (0,))) for x in split(c_ref[...])]
    want = jnp.concatenate([want[0] * 64.0 + want[1]] * 6, axis=0)

    _, _, part_tall = places((128, 20), 0)
    column = lax.broadcasted_iota(jnp.int32, (128, 20), 1)
    slots = []
    for x in split(near_ref[...]):
        for s in range(5):
            pick = (column == 5 * part_tall + s).astype(jnp.float32).astype(jnp.bfloat16)
            slots.append(exact(pick, x, ((1,), (0,))).astype(jnp.bfloat16))
    slots = jnp.concatenate(slots, axis=0)

    cols = jnp.zeros((48, 1280), jnp.float32)
    d = jnp.zeros((48, 128), jnp.int32)
    wide = jnp.concatenate([k_of] * 10, axis=1)
    for t in range(5):
        ids = jnp.concatenate([l_ref[:, 5 * g + t : 5 * g + t + 1] for g in range(6)], axis=0)
        hot = ids - start == lax.broadcasted_iota(jnp.int32, (48, near_ref.shape[1]), 1)
        hot = hot.astype(jnp.float32).astype(jnp.bfloat16)
        cols = jnp.where(wide == t, exact(hot, slots, ((1,), (1,))), cols)
        d = jnp.where(k_of == t, ids - first, d)

    remote = (part >> 1) != h
    inside = (d >= 0) & (d < 2 * HALF)
    piece = jnp.where(inside, (d >> 4) ^ h ^ 1, 2) * (2 * TILES)
    j = d & (HALF - 1)
    where = jnp.full((48, 128), ZERO, jnp.int32)
    for s in range(5):
        packed = 4 * j + s if s < 4 else 2 * TILES - HALF + j
        place = jnp.where(remote, piece + packed, jnp.where(inside, 6 * d + s, RAW + packed))
        got = cols[:, 128 * s : 128 * s + 128] * 64.0 + cols[:, 640 + 128 * s : 768 + 128 * s]
        where = jnp.where(got == want, place, where)
    tab_ref[...] = where ^ (m_of & 1)


def table(h, r, l_index, s_cols, c_index):
    total = s_cols.shape[0]
    first = 2 * HALF * r
    start = jnp.clip(first - HALF, 0, total - 4 * HALF)
    near = lax.dynamic_slice_in_dim(s_cols, start, 4 * HALF, axis=0).T
    vmem = pl.BlockSpec(memory_space=pltpu.VMEM)
    out = pl.pallas_call(
        table_body,
        out_shape=jax.ShapeDtypeStruct((48, 128), jnp.int32),
        in_specs=[pl.BlockSpec(memory_space=pltpu.SMEM), vmem, vmem, vmem],
        out_specs=vmem,
        compiler_params=pltpu.CompilerParams(vmem_limit_bytes=8 << 20),
        cost_estimate=pl.CostEstimate(flops=1 << 28, bytes_accessed=8 << 20, transcendentals=0),
    )(jnp.stack([start, first, h]), near, l_index, c_index)
    return out.reshape(48 * 128)


def shards(l_blocks, s_blocks, l_index, s_cols, c_index):
    r, c = lax.axis_index("rows"), lax.axis_index("cols")
    groups = lax.axis_size("rows")
    h = c // 2
    across = functools.partial(lax.ppermute, axis_name="cols", perm=[(k, k ^ 2) for k in range(4)])
    beside = functools.partial(lax.ppermute, axis_name="cols", perm=[(k, k ^ 1) for k in range(4)])
    up = [(4 * g + k, 4 * g + 4 + k) for g in range(groups - 1) for k in (0, 1)]
    down = [(4 * g + k, 4 * g - 4 + k) for g in range(1, groups) for k in (2, 3)]
    below, above = groups // 2 - 1, groups // 2
    seam = [(4 * below + 2 + k, 4 * above + k) for k in (0, 1)]
    seam += [(4 * above + k, 4 * below + 2 + k) for k in (0, 1)]
    plain = [route for route in up + down if route[1] not in {q for _, q in seam}]
    takes = ((r == above) & (h == 0)) | ((r == below) & (h == 1))

    def send(x, perm):
        return lax.ppermute(x, ("rows", "cols"), perm)

    first, second = pack(h.reshape(1), s_blocks)
    far_first = across(first)
    halo = send(second, up + down)
    seam_halo = send(first, seam)
    mate, first = lax.optimization_barrier((s_blocks, first))
    mate = beside(mate)
    tab = table(h, r, l_index, s_cols, c_index)
    far_first, tab = lax.optimization_barrier((far_first, tab))
    far_halo = send(far_first, plain)
    cross_first = beside(far_first)
    halo, far_first = lax.optimization_barrier((halo, far_first))
    mate_halo = beside(halo)
    parts = [(c ^ flip).reshape(1) for flip in range(4)]
    out = product(tab, parts[0], l_blocks, (s_blocks, halo), None)
    out, mate, seam_halo, second = lax.optimization_barrier((out, mate, seam_halo, second))
    far_second = across(second)
    out = product(tab, parts[1], l_blocks, (mate, mate_halo), out)
    out, far_second, far_halo = lax.optimization_barrier((out, far_second, far_halo))
    cross_second = beside(far_second)
    far_halo = jnp.where(takes, seam_halo, far_halo)
    cross_halo = beside(far_halo)
    out = product(tab, parts[2], l_blocks, (far_first, far_second, far_halo), out)
    return product(tab, parts[3], l_blocks, (cross_first, cross_second, cross_halo), out)


def solution(mesh):
    return jax.shard_map(
        shards,
        mesh=mesh,
        in_specs=(
            P(("rows", "cols"), None, None),
            P("rows", None, "cols"),
            P(("rows", "cols"), None),
            P(),
            P(("rows", "cols"), None),
        ),
        out_specs=P(("rows", "cols"), None, None),
        check_vma=False,
    )
```

```python
import functools

import jax
import jax.numpy as jnp
from jax import lax
from jax.experimental import pallas as pl
from jax.experimental.pallas import tpu as pltpu
from jax.sharding import PartitionSpec as P

HALF = 16
TILES = 40
RAW = 6 * 2 * HALF
ZERO = RAW + 2 * TILES


def pack_body(start_ref, s_ref, first_ref, second_ref):
    def row(j, carry):
        for out_ref, base in places:
            for t in range(2):
                out_ref[2 * j + t] = s_ref[base + j, :, 128 * t : 128 * t + 128]
        return carry

    def pair(j, carry):
        for out_ref, base in places:
            out_ref[32 + j] = jnp.concatenate(
                [s_ref[base + 2 * j, :, 256:320], s_ref[base + 2 * j + 1, :, 256:320]], axis=1
            )
        return carry

    places = ((first_ref, HALF * start_ref[0]), (second_ref, HALF * (1 - start_ref[0])))
    lax.fori_loop(0, HALF, row, 0, unroll=4)
    lax.fori_loop(0, HALF // 2, pair, 0, unroll=4)


def pack(start, s_blocks):
    piece = jax.ShapeDtypeStruct((TILES, 64, 128), jnp.bfloat16)
    vmem = pl.BlockSpec(memory_space=pltpu.VMEM)
    return pl.pallas_call(
        pack_body,
        out_shape=(piece, piece),
        in_specs=[pl.BlockSpec(memory_space=pltpu.SMEM), vmem],
        out_specs=(vmem,) * 2,
        compiler_params=pltpu.CompilerParams(vmem_limit_bytes=16 << 20),
        cost_estimate=pl.CostEstimate(flops=0, bytes_accessed=3 << 20, transcendentals=0),
    )(start, s_blocks)


def product_body(count, tab_ref, part_ref, l_ref, *rest):
    o_ref, sd_ref, ob_ref, sem = rest[-4:]
    rows = l_ref.shape[0]
    base = 0
    for piece in rest[:count]:
        packed = piece.shape[2] == 128

        def spread(t, carry, piece=piece, base=base, packed=packed):
            for u in range(1 if packed else 2):
                v = piece[t, :, 128 * u : 128 * u + 128]
                at = base + 2 * t if packed else base + 6 * t + 2 * u
                sd_ref[at] = v
                sd_ref[at + 1] = jnp.concatenate([v[:, 64:], v[:, :64]], axis=1)
            if not packed:
                v = piece[t, :, 256:320]
                v = jnp.concatenate([v, v], axis=1)
                sd_ref[base + 6 * t + 4] = v
                sd_ref[base + 6 * t + 5] = v
            return carry

        lax.fori_loop(0, piece.shape[0], spread, 0, unroll=8 if packed else 4)
        base += 2 * TILES if packed else RAW
    for zero in (ZERO, ZERO + 1):
        sd_ref[zero] = jnp.zeros((64, 128), jnp.bfloat16)
    part = part_ref[0]
    low = lax.broadcasted_iota(jnp.int32, (64, 128), 1) < 64

    def out(i):
        lanes = pl.ds(pl.multiple_of(part * 384, 128), 384)
        return pltpu.make_async_copy(ob_ref.at[i], o_ref.at[i, :, lanes], sem.at[i])

    def row(i, carry):
        def pick(k, m):
            at = (k // 5 * 8 + i) * 128 + k % 5 * 24 + part * 6 + 2 * m
            return jnp.where(low, sd_ref[tab_ref[at]], sd_ref[tab_ref[at + 1]])

        total = jnp.zeros((64, 384), jnp.float32)
        for k0 in range(0, 30, 4):
            ks = range(k0, min(k0 + 4, 30))
            picked = jnp.concatenate(
                [jnp.concatenate([pick(k, m) for m in range(3)], axis=1) for k in ks], axis=0
            )
            total = total + jnp.dot(
                l_ref[i, :, 64 * k0 : 64 * (k0 + len(ks))], picked, preferred_element_type=jnp.float32
            )
        ob_ref[i] = total.astype(o_ref.dtype)
        out(i).start()
        return carry

    lax.fori_loop(0, rows, row, 0, unroll=True)

    def finish(i, carry):
        out(i).wait()
        return carry

    lax.fori_loop(0, rows, finish, 0)


def product(tab, part, l_blocks, pieces, prev):
    rows = l_blocks.shape[0]
    vmem, smem = pl.BlockSpec(memory_space=pltpu.VMEM), pl.BlockSpec(memory_space=pltpu.SMEM)
    in_specs = [smem, smem] + [vmem] * (1 + len(pieces))
    args = [tab, part, l_blocks, *pieces]
    aliases = {}
    if prev is not None:
        in_specs.append(pl.BlockSpec(memory_space=pl.ANY))
        aliases = {len(args): 0}
        args.append(prev)
    return pl.pallas_call(
        functools.partial(product_body, len(pieces)),
        out_shape=jax.ShapeDtypeStruct((rows, 64, 1536), jnp.bfloat16),
        in_specs=in_specs,
        out_specs=pl.BlockSpec(memory_space=pl.ANY),
        scratch_shapes=[
            pltpu.VMEM((ZERO + 2, 64, 128), jnp.bfloat16),
            pltpu.VMEM((rows, 64, 384), jnp.bfloat16),
            pltpu.SemaphoreType.DMA((rows,)),
        ],
        input_output_aliases=aliases,
        compiler_params=pltpu.CompilerParams(vmem_limit_bytes=24 << 20),
        cost_estimate=pl.CostEstimate(flops=755_000_000, bytes_accessed=20 << 20, transcendentals=0),
    )(*args)


def split(v):
    return [x.astype(jnp.float32).astype(jnp.bfloat16) for x in (v >> 6, v & 63)]


def exact(a, b, dims):
    return lax.dot_general(a, b, (dims, ((), ())), preferred_element_type=jnp.float32)


def table_body(at_ref, near_ref, l_ref, c_ref, tab_ref):
    start, first, h = at_ref[0], at_ref[1], at_ref[2]

    def places(shape, dim):
        lane = lax.broadcasted_iota(jnp.int32, shape, dim)
        k = sum((lane >= 24 * t).astype(jnp.int32) for t in range(1, 5))
        m = lane - 24 * k
        return k, m, sum((m >= 6 * t).astype(jnp.int32) for t in range(1, 4))

    k_of, m_of, part = places((48, 128), 1)
    _, m_wide, _ = places((24, 128), 1)
    tile = (lax.broadcasted_iota(jnp.int32, (24, 128), 0) == m_wide).astype(jnp.float32).astype(jnp.bfloat16)
    want = [exact(x, tile, ((1,), (0,))) for x in split(c_ref[...])]
    want = jnp.concatenate([want[0] * 64.0 + want[1]] * 6, axis=0)

    _, _, part_tall = places((128, 20), 0)
    column = lax.broadcasted_iota(jnp.int32, (128, 20), 1)
    slots = []
    for x in split(near_ref[...]):
        for s in range(5):
            pick = (column == 5 * part_tall + s).astype(jnp.float32).astype(jnp.bfloat16)
            slots.append(exact(pick, x, ((1,), (0,))).astype(jnp.bfloat16))
    slots = jnp.concatenate(slots, axis=0)

    cols = jnp.zeros((48, 1280), jnp.float32)
    d = jnp.zeros((48, 128), jnp.int32)
    wide = jnp.concatenate([k_of] * 10, axis=1)
    for t in range(5):
        ids = jnp.concatenate([l_ref[:, 5 * g + t : 5 * g + t + 1] for g in range(6)], axis=0)
        hot = ids - start == lax.broadcasted_iota(jnp.int32, (48, near_ref.shape[1]), 1)
        hot = hot.astype(jnp.float32).astype(jnp.bfloat16)
        cols = jnp.where(wide == t, exact(hot, slots, ((1,), (1,))), cols)
        d = jnp.where(k_of == t, ids - first, d)

    remote = (part >> 1) != h
    inside = (d >= 0) & (d < 2 * HALF)
    piece = jnp.where(inside, (d >> 4) ^ h ^ 1, 2) * (2 * TILES)
    j = d & (HALF - 1)
    where = jnp.full((48, 128), ZERO, jnp.int32)
    for s in range(5):
        packed = 4 * j + s if s < 4 else 2 * TILES - HALF + j
        place = jnp.where(remote, piece + packed, jnp.where(inside, 6 * d + s, RAW + packed))
        got = cols[:, 128 * s : 128 * s + 128] * 64.0 + cols[:, 640 + 128 * s : 768 + 128 * s]
        where = jnp.where(got == want, place, where)
    tab_ref[...] = where ^ (m_of & 1)


def table(h, r, l_index, s_cols, c_index):
    total = s_cols.shape[0]
    first = 2 * HALF * r
    start = jnp.clip(first - HALF, 0, total - 4 * HALF)
    near = lax.dynamic_slice_in_dim(s_cols, start, 4 * HALF, axis=0).T
    vmem = pl.BlockSpec(memory_space=pltpu.VMEM)
    out = pl.pallas_call(
        table_body,
        out_shape=jax.ShapeDtypeStruct((48, 128), jnp.int32),
        in_specs=[pl.BlockSpec(memory_space=pltpu.SMEM), vmem, vmem, vmem],
        out_specs=vmem,
        compiler_params=pltpu.CompilerParams(vmem_limit_bytes=8 << 20),
        cost_estimate=pl.CostEstimate(flops=1 << 28, bytes_accessed=8 << 20, transcendentals=0),
    )(jnp.stack([start, first, h]), near, l_index, c_index)
    return out.reshape(48 * 128)


def shards(l_blocks, s_blocks, l_index, s_cols, c_index):
    r, c = lax.axis_index("rows"), lax.axis_index("cols")
    groups = lax.axis_size("rows")
    h = c // 2
    across = functools.partial(lax.ppermute, axis_name="cols", perm=[(k, k ^ 2) for k in range(4)])
    beside = functools.partial(lax.ppermute, axis_name="cols", perm=[(k, k ^ 1) for k in range(4)])
    up = [(4 * g + k, 4 * g + 4 + k) for g in range(groups - 1) for k in (0, 1)]
    down = [(4 * g + k, 4 * g - 4 + k) for g in range(1, groups) for k in (2, 3)]
    below, above = groups // 2 - 1, groups // 2
    seam = [(4 * below + 2 + k, 4 * above + k) for k in (0, 1)]
    seam += [(4 * above + k, 4 * below + 2 + k) for k in (0, 1)]
    plain = [route for route in up + down if route[1] not in {q for _, q in seam}]
    takes = ((r == above) & (h == 0)) | ((r == below) & (h == 1))

    def send(x, perm):
        return lax.ppermute(x, ("rows", "cols"), perm)

    first, second = pack(h.reshape(1), s_blocks)
    far_first = across(first)
    halo = send(second, up + down)
    mate, first = lax.optimization_barrier((s_blocks, first))
    mate = beside(mate)
    tab = table(h, r, l_index, s_cols, c_index)
    second, far_first, tab = lax.optimization_barrier((second, far_first, tab))
    far_second = across(second)
    far_halo = send(far_first, plain)
    cross_first = beside(far_first)
    halo, far_first, first = lax.optimization_barrier((halo, far_first, first))
    seam_halo = send(first, seam)
    mate_halo = beside(halo)
    parts = [(c ^ flip).reshape(1) for flip in range(4)]
    out = product(tab, parts[0], l_blocks, (s_blocks, halo), None)
    out, mate = lax.optimization_barrier((out, mate))
    out = product(tab, parts[1], l_blocks, (mate, mate_halo), out)
    out, far_second, far_halo, seam_halo = lax.optimization_barrier((out, far_second, far_halo, seam_halo))
    cross_second = beside(far_second)
    far_halo = jnp.where(takes, seam_halo, far_halo)
    cross_halo = beside(far_halo)
    out = product(tab, parts[2], l_blocks, (far_first, far_second, far_halo), out)
    return product(tab, parts[3], l_blocks, (cross_first, cross_second, cross_halo), out)


def solution(mesh):
    return jax.shard_map(
        shards,
        mesh=mesh,
        in_specs=(
            P(("rows", "cols"), None, None),
            P("rows", None, "cols"),
            P(("rows", "cols"), None),
            P(),
            P(("rows", "cols"), None),
        ),
        out_specs=P(("rows", "cols"), None, None),
        check_vma=False,
    )
```

```python
import functools

import jax
import jax.numpy as jnp
from jax import lax
from jax.experimental import pallas as pl
from jax.experimental.pallas import tpu as pltpu
from jax.sharding import PartitionSpec as P

HALF = 16
TILES = 40
RAW = 6 * 2 * HALF
ZERO = RAW + 2 * TILES


def pack_body(start_ref, s_ref, first_ref, second_ref):
    def row(j, carry):
        for out_ref, base in places:
            for t in range(2):
                out_ref[2 * j + t] = s_ref[base + j, :, 128 * t : 128 * t + 128]
        return carry

    def pair(j, carry):
        for out_ref, base in places:
            out_ref[32 + j] = jnp.concatenate(
                [s_ref[base + 2 * j, :, 256:320], s_ref[base + 2 * j + 1, :, 256:320]], axis=1
            )
        return carry

    places = ((first_ref, HALF * start_ref[0]), (second_ref, HALF * (1 - start_ref[0])))
    lax.fori_loop(0, HALF, row, 0, unroll=4)
    lax.fori_loop(0, HALF // 2, pair, 0, unroll=4)


def pack(start, s_blocks):
    piece = jax.ShapeDtypeStruct((TILES, 64, 128), jnp.bfloat16)
    vmem = pl.BlockSpec(memory_space=pltpu.VMEM)
    return pl.pallas_call(
        pack_body,
        out_shape=(piece, piece),
        in_specs=[pl.BlockSpec(memory_space=pltpu.SMEM), vmem],
        out_specs=(vmem,) * 2,
        compiler_params=pltpu.CompilerParams(vmem_limit_bytes=16 << 20),
        cost_estimate=pl.CostEstimate(flops=0, bytes_accessed=3 << 20, transcendentals=0),
    )(start, s_blocks)


def product_body(count, tab_ref, part_ref, l_ref, *rest):
    o_ref, sd_ref, ob_ref, sem = rest[-4:]
    rows = l_ref.shape[0]
    base = 0
    for piece in rest[:count]:
        packed = piece.shape[2] == 128

        def spread(t, carry, piece=piece, base=base, packed=packed):
            for u in range(1 if packed else 2):
                v = piece[t, :, 128 * u : 128 * u + 128]
                at = base + 2 * t if packed else base + 6 * t + 2 * u
                sd_ref[at] = v
                sd_ref[at + 1] = jnp.concatenate([v[:, 64:], v[:, :64]], axis=1)
            if not packed:
                v = piece[t, :, 256:320]
                v = jnp.concatenate([v, v], axis=1)
                sd_ref[base + 6 * t + 4] = v
                sd_ref[base + 6 * t + 5] = v
            return carry

        lax.fori_loop(0, piece.shape[0], spread, 0, unroll=8 if packed else 4)
        base += 2 * TILES if packed else RAW
    for zero in (ZERO, ZERO + 1):
        sd_ref[zero] = jnp.zeros((64, 128), jnp.bfloat16)
    part = part_ref[0]
    low = lax.broadcasted_iota(jnp.int32, (64, 128), 1) < 64

    def out(i):
        lanes = pl.ds(pl.multiple_of(part * 384, 128), 384)
        return pltpu.make_async_copy(ob_ref.at[i], o_ref.at[i, :, lanes], sem.at[i])

    def row(i, carry):
        def pick(k, m):
            at = (k // 5 * 8 + i) * 128 + k % 5 * 24 + part * 6 + 2 * m
            return jnp.where(low, sd_ref[tab_ref[at]], sd_ref[tab_ref[at + 1]])

        total = jnp.zeros((64, 384), jnp.float32)
        for k0 in range(0, 30, 4):
            ks = range(k0, min(k0 + 4, 30))
            picked = jnp.concatenate(
                [jnp.concatenate([pick(k, m) for m in range(3)], axis=1) for k in ks], axis=0
            )
            total = total + jnp.dot(
                l_ref[i, :, 64 * k0 : 64 * (k0 + len(ks))], picked, preferred_element_type=jnp.float32
            )
        ob_ref[i] = total.astype(o_ref.dtype)
        out(i).start()
        return carry

    lax.fori_loop(0, rows, row, 0, unroll=True)

    def finish(i, carry):
        out(i).wait()
        return carry

    lax.fori_loop(0, rows, finish, 0)


def product(tab, part, l_blocks, pieces, prev):
    rows = l_blocks.shape[0]
    vmem, smem = pl.BlockSpec(memory_space=pltpu.VMEM), pl.BlockSpec(memory_space=pltpu.SMEM)
    in_specs = [smem, smem] + [vmem] * (1 + len(pieces))
    args = [tab, part, l_blocks, *pieces]
    aliases = {}
    if prev is not None:
        in_specs.append(pl.BlockSpec(memory_space=pl.ANY))
        aliases = {len(args): 0}
        args.append(prev)
    return pl.pallas_call(
        functools.partial(product_body, len(pieces)),
        out_shape=jax.ShapeDtypeStruct((rows, 64, 1536), jnp.bfloat16),
        in_specs=in_specs,
        out_specs=pl.BlockSpec(memory_space=pl.ANY),
        scratch_shapes=[
            pltpu.VMEM((ZERO + 2, 64, 128), jnp.bfloat16),
            pltpu.VMEM((rows, 64, 384), jnp.bfloat16),
            pltpu.SemaphoreType.DMA((rows,)),
        ],
        input_output_aliases=aliases,
        compiler_params=pltpu.CompilerParams(vmem_limit_bytes=24 << 20),
        cost_estimate=pl.CostEstimate(flops=755_000_000, bytes_accessed=20 << 20, transcendentals=0),
    )(*args)


def split(v):
    return [x.astype(jnp.float32).astype(jnp.bfloat16) for x in (v >> 6, v & 63)]


def exact(a, b, dims):
    return lax.dot_general(a, b, (dims, ((), ())), preferred_element_type=jnp.float32)


def table_body(at_ref, near_ref, l_ref, c_ref, tab_ref):
    start, first, h = at_ref[0], at_ref[1], at_ref[2]

    def places(shape, dim):
        lane = lax.broadcasted_iota(jnp.int32, shape, dim)
        k = sum((lane >= 24 * t).astype(jnp.int32) for t in range(1, 5))
        m = lane - 24 * k
        return k, m, sum((m >= 6 * t).astype(jnp.int32) for t in range(1, 4))

    k_of, m_of, part = places((48, 128), 1)
    _, m_wide, _ = places((24, 128), 1)
    tile = (lax.broadcasted_iota(jnp.int32, (24, 128), 0) == m_wide).astype(jnp.float32).astype(jnp.bfloat16)
    want = [exact(x, tile, ((1,), (0,))) for x in split(c_ref[...])]
    want = jnp.concatenate([want[0] * 64.0 + want[1]] * 6, axis=0)

    _, _, part_tall = places((128, 20), 0)
    column = lax.broadcasted_iota(jnp.int32, (128, 20), 1)
    slots = []
    for x in split(near_ref[...]):
        for s in range(5):
            pick = (column == 5 * part_tall + s).astype(jnp.float32).astype(jnp.bfloat16)
            slots.append(exact(pick, x, ((1,), (0,))).astype(jnp.bfloat16))
    slots = jnp.concatenate(slots, axis=0)

    cols = jnp.zeros((48, 1280), jnp.float32)
    d = jnp.zeros((48, 128), jnp.int32)
    wide = jnp.concatenate([k_of] * 10, axis=1)
    for t in range(5):
        ids = jnp.concatenate([l_ref[:, 5 * g + t : 5 * g + t + 1] for g in range(6)], axis=0)
        hot = ids - start == lax.broadcasted_iota(jnp.int32, (48, near_ref.shape[1]), 1)
        hot = hot.astype(jnp.float32).astype(jnp.bfloat16)
        cols = jnp.where(wide == t, exact(hot, slots, ((1,), (1,))), cols)
        d = jnp.where(k_of == t, ids - first, d)

    remote = (part >> 1) != h
    inside = (d >= 0) & (d < 2 * HALF)
    piece = jnp.where(inside, (d >> 4) ^ h ^ 1, 2) * (2 * TILES)
    j = d & (HALF - 1)
    where = jnp.full((48, 128), ZERO, jnp.int32)
    for s in range(5):
        packed = 4 * j + s if s < 4 else 2 * TILES - HALF + j
        place = jnp.where(remote, piece + packed, jnp.where(inside, 6 * d + s, RAW + packed))
        got = cols[:, 128 * s : 128 * s + 128] * 64.0 + cols[:, 640 + 128 * s : 768 + 128 * s]
        where = jnp.where(got == want, place, where)
    tab_ref[...] = where ^ (m_of & 1)


def table(h, r, l_index, s_cols, c_index):
    total = s_cols.shape[0]
    first = 2 * HALF * r
    start = jnp.clip(first - HALF, 0, total - 4 * HALF)
    near = lax.dynamic_slice_in_dim(s_cols, start, 4 * HALF, axis=0).T
    vmem = pl.BlockSpec(memory_space=pltpu.VMEM)
    out = pl.pallas_call(
        table_body,
        out_shape=jax.ShapeDtypeStruct((48, 128), jnp.int32),
        in_specs=[pl.BlockSpec(memory_space=pltpu.SMEM), vmem, vmem, vmem],
        out_specs=vmem,
        compiler_params=pltpu.CompilerParams(vmem_limit_bytes=8 << 20),
        cost_estimate=pl.CostEstimate(flops=1 << 28, bytes_accessed=8 << 20, transcendentals=0),
    )(jnp.stack([start, first, h]), near, l_index, c_index)
    return out.reshape(48 * 128)


def shards(l_blocks, s_blocks, l_index, s_cols, c_index):
    r, c = lax.axis_index("rows"), lax.axis_index("cols")
    groups = lax.axis_size("rows")
    h = c // 2
    across = functools.partial(lax.ppermute, axis_name="cols", perm=[(k, k ^ 2) for k in range(4)])
    beside = functools.partial(lax.ppermute, axis_name="cols", perm=[(k, k ^ 1) for k in range(4)])
    up = [(4 * g + k, 4 * g + 4 + k) for g in range(groups - 1) for k in (0, 1)]
    down = [(4 * g + k, 4 * g - 4 + k) for g in range(1, groups) for k in (2, 3)]
    below, above = groups // 2 - 1, groups // 2
    seam = [(4 * below + 2 + k, 4 * above + k) for k in (0, 1)]
    seam += [(4 * above + k, 4 * below + 2 + k) for k in (0, 1)]
    plain = [route for route in up + down if route[1] not in {q for _, q in seam}]
    takes = ((r == above) & (h == 0)) | ((r == below) & (h == 1))

    def send(x, perm):
        return lax.ppermute(x, ("rows", "cols"), perm)

    first, second = pack(h.reshape(1), s_blocks)
    far_first = across(first)
    halo = send(second, up + down)
    seam_halo = send(first, seam)
    mate, first = lax.optimization_barrier((s_blocks, first))
    mate = beside(mate)
    tab = table(h, r, l_index, s_cols, c_index)
    second, halo, tab = lax.optimization_barrier((second, halo, tab))
    far_second = across(second)

    far_halo = send(far_first, plain)
    cross_first = beside(far_first)
    mate_halo = beside(halo)
    tab, far_first = lax.optimization_barrier((tab, far_first))
    parts = [(c ^ flip).reshape(1) for flip in range(4)]
    out = product(tab, parts[0], l_blocks, (s_blocks, halo), None)
    out = product(tab, parts[1], l_blocks, (mate, mate_halo), out)
    out, far_second, far_halo, seam_halo = lax.optimization_barrier((out, far_second, far_halo, seam_halo))
    cross_second = beside(far_second)
    far_halo = jnp.where(takes, seam_halo, far_halo)
    cross_halo = beside(far_halo)
    out = product(tab, parts[2], l_blocks, (far_first, far_second, far_halo), out)
    return product(tab, parts[3], l_blocks, (cross_first, cross_second, cross_halo), out)


def solution(mesh):
    return jax.shard_map(
        shards,
        mesh=mesh,
        in_specs=(
            P(("rows", "cols"), None, None),
            P("rows", None, "cols"),
            P(("rows", "cols"), None),
            P(),
            P(("rows", "cols"), None),
        ),
        out_specs=P(("rows", "cols"), None, None),
        check_vma=False,
    )
```
